32 devices in a mesh: slides: 2 (over y), rows: 4 (over z), cols: 2 (over x), chan: 2 (over core).
Axes of the slice: x: 2, y: 2, z: 4, core: 2. Of those that a mesh axis runs over, the one named last changes fastest.
Arguments:
- features: bfloat16 [128, 64, 384], P(('slides', 'rows'), 'cols', 'chan'), parts along dimension 0, may hold values from -6 to 6
- gate_input: bfloat16 [128, 64, 384], P(('slides', 'rows'), 'cols', 'chan'), parts along dimension 0, may hold values from -6 to 6
- decay_idx: int32 [128, 64], P(('slides', 'rows'), 'cols'), parts along dimension 0, may hold values from 0 to 15
- log_table: float32 [16, 384], P(None, 'chan'), may hold values from -1 to 0, as said below
- state_rate: float32 [16], replicated, may hold values from 0.5 to 2
- proj_row: bfloat16 [384, 32], P('chan'), may hold values from -0.0390625 to 0.0390625
- proj_col: bfloat16 [384, 32], P('chan'), may hold values from -0.0390625 to 0.0390625
- conv_w: float32 [3, 3, 384], P(None, None, 'chan'), may hold values from -0.5 to 0.5
- conv_b: float32 [384], P('chan'), may hold values from -0.5 to 0.5
- d_skip: float32 [384], P('chan'), may hold values from 0.5 to 1.5
Outputs:
- output: bfloat16 [128, 64, 384], P(('slides', 'rows'), 'cols', 'chan'), parts along dimension 0
The draws below stay inside these ranges and needn't reach their ends.
There are 2 independent parts, one for each index of `slides`. The reference program is written for one: setup_inputs(seed, part) draws one part's arguments, and reference() takes and returns one part's arrays. A program takes and returns all parts, laid end to end along the dimension named above; an argument that names none is the same for every part. Nothing has to cross between parts.
Inputs may be any that keep to these rules, and one draw needn't show every extreme that they name: `log_table`: every entry is negative.
All inputs are finite; a program needn't handle non-finite values.
Results may differ from the reference program's by a relative error of at most 0.0061.
Values may be sent and summed in bfloat16 or wider, within the bound.
No kernel may reach another device: no remote copies, remote signals or barrier semaphores. Data moves between devices by JAX's collectives and lax.ppermute only.
A program may use at most 128 MiB of HBM per device.

```python
import math
import jax
import jax.numpy as jnp
from jax import lax

INNER_WIDTH = 384
S = 16
K = 16
PATCH_ROWS = 64
PATCH_COLUMNS = 64


def draw_log_table(key, part):
    key_mask = jax.random.fold_in(key, 11)
    key_slow = jax.random.fold_in(key, 12)
    key_quick = jax.random.fold_in(key, 13)
    key_factor = jax.random.fold_in(key, 14)
    spike_key = jax.random.fold_in(key, 15)
    share = 0.5
    quick_mask = jax.random.uniform(key_mask, (INNER_WIDTH,), jnp.float32) < share
    slow_rate = jnp.exp(jax.random.uniform(key_slow, (INNER_WIDTH,), jnp.float32, minval=jnp.log(0.1 / PATCH_ROWS), maxval=jnp.log(1.0 / PATCH_ROWS)))
    quick_rate = jnp.exp(jax.random.uniform(key_quick, (INNER_WIDTH,), jnp.float32, minval=jnp.log(1.0 / 50.0), maxval=jnp.log(1.0 / 30.0)))
    baseline_rate = jnp.where(quick_mask, quick_rate, slow_rate)
    factors = jnp.exp(jax.random.uniform(key_factor, (K - 1, INNER_WIDTH), jnp.float32, minval=jnp.log(0.5), maxval=jnp.log(2.0)))
    spike_penalty = -jnp.log(jax.random.uniform(spike_key, (INNER_WIDTH,), jnp.float32, minval=0.5, maxval=0.8))
    leading_row = baseline_rate + spike_penalty
    table = jnp.concatenate([leading_row[None, :], baseline_rate[None, :] * factors], axis=0)
    return (-table).astype(jnp.float32)


def draw_decay_idx(key, part):
    key_levels = jax.random.fold_in(key, 21)
    spike_key = jax.random.fold_in(key, 22)
    level_values = jax.random.randint(key_levels, (PATCH_ROWS, PATCH_COLUMNS), 1, K)
    spike_sample = jax.random.randint(spike_key, (PATCH_ROWS, PATCH_COLUMNS), 0, 256)
    return jnp.where(spike_sample == 0, 0, level_values).astype(jnp.int32)


def levels(stream_key, extent, shards, least, largest):
    def one(axis_at, shards_of):
        heights = jax.random.uniform(jax.random.fold_in(jax.random.fold_in(stream_key, 6), axis_at), (shards_of,), jnp.float32, least / len(shards), largest / len(shards))
        return jnp.repeat(jnp.exp(heights), extent[axis_at] // shards_of).reshape((-1,) + (1,) * (len(extent) - axis_at - 1))

    level = one(*shards[0])
    for cut in shards[1:]:
        level = level * one(*cut)
    return level


def gaussian(own_key, dims, deviation, limit, shards=(), held_as=jnp.bfloat16):
    loudness = levels(own_key, dims, shards, -0.22, 0.18) if shards else 1.0
    array = jax.random.normal(own_key, dims, jnp.float32) * deviation * loudness
    return jnp.minimum(jnp.maximum(array, -limit), limit).astype(held_as)


def setup_inputs(seed: int = 0, part: int = 0) -> dict:
    seeds = jax.random.split(jax.random.key(seed), 11)
    own_keys = jax.random.split(jax.random.fold_in(seeds[10], part), 11)
    return {
        "features": gaussian(own_keys[0], (PATCH_ROWS, PATCH_COLUMNS, INNER_WIDTH), 1.0, 6.0, ((0, 4), (1, 2), (2, 2))),
        "gate_input": gaussian(own_keys[1], (PATCH_ROWS, PATCH_COLUMNS, INNER_WIDTH), 1.0, 6.0, ((0, 4), (1, 2), (2, 2))),
        "decay_idx": draw_decay_idx(jax.random.fold_in(jax.random.fold_in(seeds[10], part), 71), part),
        "log_table": draw_log_table(jax.random.fold_in(seeds[10], 71), part),
        "state_rate": jnp.clip(jnp.exp(jax.random.uniform(seeds[4], (S,), jnp.float32, math.log(0.5), math.log(2.0))), 0.5, 2.0),
        "proj_row": gaussian(seeds[5], (INNER_WIDTH, 2 * S), (64 * INNER_WIDTH) ** -0.5, 0.0390625, ((0, 2),)),
        "proj_col": gaussian(seeds[6], (INNER_WIDTH, 2 * S), (64 * INNER_WIDTH) ** -0.5, 0.0390625, ((0, 2),)),
        "conv_w": jnp.clip(jax.random.uniform(seeds[7], (3, 3, INNER_WIDTH), jnp.float32, -0.5, 0.5) * levels(seeds[7], (3, 3, INNER_WIDTH), ((2, 2),), -0.4, 0.0), -0.5, 0.5),
        "conv_b": jnp.clip(jax.random.uniform(seeds[8], (INNER_WIDTH,), jnp.float32, -0.5, 0.5) * levels(seeds[8], (INNER_WIDTH,), ((0, 2),), -0.4, 0.0), -0.5, 0.5),
        "d_skip": jnp.clip(0.5 + 1.0 * jax.random.uniform(seeds[9], (INNER_WIDTH,), jnp.float32) ** levels(seeds[9], (INNER_WIDTH,), ((0, 2),), -0.2, 0.2), 0.5, 1.5),
    }


def combine_pair(earlier, latter):
    return earlier[0] + latter[0], latter[1] + jnp.exp(latter[0]) * earlier[1]


def axis_scan(values, log_decays, coeffs, state_rate):
    num_states = state_rate.shape[0]

    def one_state(summed, which_state):
        state_scale = state_rate[which_state]
        drive_col = lax.dynamic_index_in_dim(coeffs, which_state, 2, keepdims=True)
        out_col = lax.dynamic_index_in_dim(coeffs, which_state + num_states, 2, keepdims=True)
        cumulative, states = lax.associative_scan(combine_pair, (log_decays * state_scale, drive_col * values), axis=0)
        return summed + out_col * states, None

    summed, unused = lax.scan(one_state, jnp.zeros(values.shape, jnp.float32), jnp.arange(num_states, dtype=jnp.int32))
    return summed


def reference(features, gate_input, decay_idx, log_table, state_rate, proj_row, proj_col, conv_w, conv_b, d_skip):
    log_decays = jnp.take(log_table, decay_idx, axis=0)
    feats_wide = features.astype(jnp.float32)
    coeff_row = jnp.dot(features, proj_row, preferred_element_type=jnp.float32)
    swept_rows = axis_scan(feats_wide.transpose(1, 0, 2), log_decays.transpose(1, 0, 2), coeff_row.transpose(1, 0, 2), state_rate).transpose(1, 0, 2)
    row_out = (swept_rows + d_skip * feats_wide).astype(jnp.bfloat16)
    padded = jnp.pad(row_out.astype(jnp.float32), ((1, 1), (1, 1), (0, 0)))
    convolved = jnp.zeros(feats_wide.shape, jnp.float32) + conv_b
    for offset_row in range(3):
        for offset_col in range(3):
            convolved = convolved + conv_w[offset_row, offset_col] * padded[offset_row:offset_row + PATCH_ROWS, offset_col:offset_col + PATCH_COLUMNS]
    middle = jax.nn.silu(convolved).astype(jnp.bfloat16)
    middle_wide = middle.astype(jnp.float32)
    coeff_col = jnp.dot(middle, proj_col, preferred_element_type=jnp.float32)
    combined = axis_scan(middle_wide, log_decays, coeff_col, state_rate) + d_skip * middle_wide
    return (combined * jax.nn.silu(gate_input.astype(jnp.float32))).astype(jnp.bfloat16)
```

```python
import jax
import jax.numpy as jnp
from jax import lax
from jax.experimental import pallas as pl
from jax.experimental.pallas import tpu as pltpu
from jax.sharding import PartitionSpec as P

LANES = 128
SUB = 8
LOG2E = 1.4426950408889634
F32 = jnp.float32
BF16 = jnp.bfloat16


def low_half(shape):
    return lax.broadcasted_iota(jnp.int32, shape, len(shape) - 1) < LANES // 2


def twice(v):
    return jnp.concatenate([v, v], axis=-1)


def split3(t):
    hi = t.astype(BF16)
    rest = t - hi.astype(F32)
    mid = rest.astype(BF16)
    low = (rest - mid.astype(F32)).astype(BF16)
    return jnp.concatenate([hi, mid, low], axis=0)


def tables(table_ref):
    t = table_ref[...] * LOG2E
    return split3(t[:, :LANES]), split3(twice(t[:, LANES:]))


def dot(a, b):
    return jnp.dot(a, b, preferred_element_type=F32)


def pair_rates(rate_ref, rows):
    half = low_half((rows, LANES))
    states = rate_ref.shape[0]
    return [jnp.where(half, rate_ref[2 * j], rate_ref[2 * j + 1]) for j in range(states // 2)]


def advance(carry, xa, xb, la, lb, coeff, rate_ref, rates_b, wanted):
    states = rate_ref.shape[0]
    shape = xa.shape
    half = low_half(shape)

    def spread(col):
        return jnp.broadcast_to(coeff[:, col : col + 1], shape)

    drive = [spread(s) for s in range(states)]
    out = [spread(states + s) for s in range(states)] if wanted else None
    new, ya, yb = [], [], []
    for s in range(states):
        st = jnp.exp2(la * rate_ref[s]) * carry[s] + drive[s] * xa
        new.append(st)
        if wanted:
            ya.append(out[s] * st)
    for j in range(states // 2):
        b = jnp.where(half, drive[2 * j], drive[2 * j + 1])
        st = jnp.exp2(lb * rates_b[j]) * carry[states + j] + b * xb
        new.append(st)
        if wanted:
            yb.append(jnp.where(half, out[2 * j], out[2 * j + 1]) * st)
    if not wanted:
        return tuple(new), None, None

    def tree(v):
        while len(v) > 1:
            v = [v[i] + v[i + 1] for i in range(0, len(v) - 1, 2)] + v[len(v) & ~1 :]
        return v[0]

    yb = tree(yb)
    return tuple(new), tree(ya), yb + pltpu.roll(yb, LANES // 2, 1)


def row_kernel(dims, dest, *refs):
    tiles, strips, height, width, strip = dims
    rate_ref = refs[0]
    own, other = refs[1 : 1 + tiles], refs[1 + tiles : 1 + 2 * tiles]
    hots = refs[1 + 2 * tiles : 1 + 3 * tiles]
    table_ref, proj_ref, proj2_ref, skip_ref = refs[1 + 3 * tiles : 5 + 3 * tiles]
    outs = refs[5 + 3 * tiles : 5 + 3 * tiles + strips]
    xa_ref, xb_ref, la_ref, lb_ref, cf_ref, ya_ref, yb_ref = refs[5 + 3 * tiles + strips :]
    states = rate_ref.shape[0]
    cells = height * width
    col = lax.axis_index("cols")
    row = lax.axis_index("rows")

    ta, tb = tables(table_ref)
    for d in range(tiles):
        x = own[d][...].reshape(cells, -1)
        part = pl.ds(d * cells, cells)
        cf_ref[part, : 2 * states] = dot(x, proj_ref[...]) + dot(
            other[d][...].reshape(cells, -1), proj2_ref[...]
        )
        xf = x.astype(F32)
        xa_ref[part, :] = xf[:, :LANES]
        xb_ref[part, :] = twice(xf[:, LANES:])
        hot = hots[d][...]
        la_ref[part, :] = dot(hot, ta)
        lb_ref[part, :] = dot(hot, tb)

    rates_b = pair_rates(rate_ref, SUB)
    skip = skip_ref[...]
    skip_a, skip_b = skip[:, :LANES], twice(skip[:, LANES:])
    last_left = (col >= tiles - 1).astype(F32)

    for g in range(height // SUB):

        def step(carry, d, w, scale, wanted, g=g):
            place = pl.ds(d * cells + g * SUB * width + w, SUB, stride=width)
            ordered = pl.ds(pl.multiple_of(d * cells + w * height + g * SUB, SUB), SUB)
            xa, xb = xa_ref[place, :], xb_ref[place, :]
            if scale is not None:
                xa, xb = xa * scale, xb * scale
            carry, ya, yb = advance(
                carry, xa, xb, la_ref[ordered, :], lb_ref[ordered, :], cf_ref[place, :], rate_ref, rates_b, wanted
            )
            if wanted:
                ya, yb = ya + skip_a * xa, yb + skip_b * xb
            return carry, ya, yb

        def put(c, ya, yb, g=g):
            at = pl.ds(pl.multiple_of(c * height + g * SUB, SUB), SUB)
            ya_ref[at, :] = ya
            yb_ref[at, :] = yb

        carry = tuple(jnp.zeros((SUB, LANES), F32) for _ in range(states + states // 2))
        for d in range(tiles - 1, 0, -1):
            scale = (col >= d).astype(F32)
            carry = lax.fori_loop(
                0,
                width - (d == 1),
                lambda w, s, d=d, scale=scale: step(s, d, w, scale, False)[0],
                carry,
            )
        carry, ya, yb = step(carry, 1, width - 1, (col >= 1).astype(F32), True)
        put(0, ya, yb)

        def body(w, s):
            s, ya, yb = step(s, 0, w, None, True)
            put(w + 1, ya, yb)
            return s

        carry = lax.fori_loop(0, width, body, carry)
        _, ya, yb = step(carry, tiles - 1, 0, None, True)
        inside = 1.0 - last_left
        put(width + 1, ya * inside, yb * inside)

    count = strip + 2
    for d in range(strips):
        start = pl.multiple_of(dest(row, d) * strip * height, SUB)
        from_ = pl.ds(start, count * height)
        outs[d][: count * height, :] = ya_ref[from_, :].astype(BF16)
        yb = yb_ref[from_, :].reshape(count, 2, height // 2, LANES)
        low, high = yb[:, 0], yb[:, 1]
        packed = jnp.where(low_half(low.shape), low, high).reshape(count * height // 2, LANES)
        outs[d][count * height :, :] = packed.astype(BF16)


def unpack(v):
    half = low_half(v.shape)
    turned = pltpu.roll(v, LANES // 2, 1)
    return jnp.where(half, v, turned), jnp.where(half, turned, v)


def column_kernel(dims, dest, *refs):
    strips, height, strip = dims
    rate_ref = refs[0]
    blocks = (refs[1 : 1 + strips], refs[1 + strips : 1 + 2 * strips])
    at = 1 + 2 * strips
    hot_ref, table_ref = refs[at : at + 2]
    projs = refs[at + 2 : at + 4]
    conv_ws = refs[at + 4 : at + 6]
    conv_bs = refs[at + 6 : at + 8]
    skip_ref = refs[at + 8]
    outs = refs[at + 9 : at + 9 + strips]
    ra_ref, rb_ref, ma_ref, mb_ref, la_ref, lb_ref, cf_ref, ya_ref, yb_ref = refs[at + 9 + strips :]
    states = rate_ref.shape[0]
    row = lax.axis_index("rows")
    total = strips * height
    pitch = total + 2 * SUB
    count = strip + 2

    ta, tb = tables(table_ref)
    hot = hot_ref[...]
    la_ref[...] = dot(hot, ta)
    lb_ref[...] = dot(hot, tb)
    zero = jnp.zeros((SUB, LANES), F32)
    for k in range(count):
        for ref in (ra_ref, rb_ref):
            ref[pl.ds(k * pitch, SUB), :] = zero
            ref[pl.ds(k * pitch + SUB + total, SUB), :] = zero

    coeff = None
    for side in (1, 0):
        for d in range(strips):
            base = pl.multiple_of(dest(row, d) * height, SUB) + SUB
            va = blocks[side][d][: count * height, :].astype(F32)
            low, high = unpack(blocks[side][d][count * height :, :].astype(F32))
            h2 = height // 2
            for k in range(count):
                to = pl.multiple_of(base + k * pitch, SUB)
                ra_ref[pl.ds(to, height), :] = va[k * height : (k + 1) * height]
                rb_ref[pl.ds(to, h2), :] = low[k * h2 : (k + 1) * h2]
                rb_ref[pl.ds(pl.multiple_of(to + h2, SUB), h2), :] = high[k * h2 : (k + 1) * h2]
        taps = conv_ws[side][...]
        bias = conv_bs[side][...]
        for src, dst, cut in (
            (ra_ref, ma_ref, lambda v: v[..., :LANES]),
            (rb_ref, mb_ref, lambda v: twice(v[..., LANES:])),
        ):
            weights, add = cut(taps), cut(bias)
            spread = [[jnp.broadcast_to(weights[a, b][None, :], (SUB, LANES)) for b in range(3)] for a in range(3)]
            start = jnp.broadcast_to(add, (SUB, LANES))

            def conv(i, unused, src=src, dst=dst, spread=spread, start=start):
                sums = [start] * strip
                for k in range(count):
                    for a in range(3):
                        v = src[pl.ds(k * pitch + i * SUB + SUB - 1 + a, SUB), :]
                        for b in range(3):
                            if 0 <= k - b < strip:
                                sums[k - b] = sums[k - b] + spread[a][b] * v
                for k in range(strip):
                    v = sums[k] / (1.0 + jnp.exp(-sums[k]))
                    dst[pl.ds(pl.multiple_of(k * total + i * SUB, SUB), SUB), :] = v.astype(BF16).astype(F32)
                return unused

            lax.fori_loop(0, total // SUB, conv, 0)
        proj = projs[side][...]
        part = dot(ma_ref[...].astype(BF16), proj[:LANES]) + dot(
            mb_ref[:, : LANES // 2].astype(BF16), proj[LANES:]
        )
        coeff = part if coeff is None else coeff + part
    cf_ref[:, : 2 * states] = coeff

    rates_b = pair_rates(rate_ref, strip)
    skip = skip_ref[...]
    skip_a, skip_b = skip[:, :LANES], twice(skip[:, LANES:])

    def body(h, carry):
        place = pl.ds(h, strip, stride=total)
        ordered = pl.ds(h * strip if strip % SUB else pl.multiple_of(h * strip, SUB), strip)
        xa, xb = ma_ref[place, :], mb_ref[place, :]
        carry, ya, yb = advance(
            carry, xa, xb, la_ref[ordered, :], lb_ref[ordered, :], cf_ref[place, :], rate_ref, rates_b, True
        )
        ya_ref[ordered, :] = ya + skip_a * xa
        yb_ref[ordered, :] = yb + skip_b * xb
        return carry

    zeros = tuple(jnp.zeros((strip, LANES), F32) for _ in range(states + states // 2))
    lax.fori_loop(0, total, body, zeros)

    cells = height * strip
    for d in range(strips):
        start = pl.multiple_of(dest(row, d) * cells, SUB)
        from_ = pl.ds(start, cells)
        outs[d][:cells, :] = ya_ref[from_, :].astype(BF16)
        yb = yb_ref[from_, :]
        low, high = yb[: cells // 2], yb[cells // 2 :]
        outs[d][cells:, :] = jnp.where(low_half(low.shape), low, high).astype(BF16)


def gate_kernel(dims, dest, *refs):
    strips, height, width, strip = dims
    blocks, gate_ref, out_ref, ya_ref, yb_ref = refs[:strips], *refs[strips:]
    row = lax.axis_index("rows")
    cells = height * strip
    for d in range(strips):
        va = blocks[d][:cells, :].astype(F32)
        low, high = unpack(blocks[d][cells:, :].astype(F32))
        left = dest(row, d) * strip
        for h in range(height):
            to = left + h * width
            to = pl.ds(to if strip % SUB else pl.multiple_of(to, SUB), strip)
            ya_ref[to, :] = va[h * strip : (h + 1) * strip]
            b, i = (low, h) if h < height // 2 else (high, h - height // 2)
            yb_ref[to, :] = b[i * strip : (i + 1) * strip]
    gate = gate_ref[...].astype(F32)
    gate = gate / (1.0 + jnp.exp(-gate))
    out_ref[:, :, :LANES] = (ya_ref[...].reshape(height, width, LANES) * gate[:, :, :LANES]).astype(BF16)
    yb = yb_ref[...].reshape(height, width, LANES)[:, :, : LANES // 2]
    out_ref[:, :, LANES:] = (yb * gate[:, :, LANES:]).astype(BF16)


def smem():
    return pl.BlockSpec(memory_space=pltpu.SMEM)


def vmem():
    return pl.BlockSpec(memory_space=pltpu.VMEM)


def call(kernel, args, outs, scratch, name):
    return pl.pallas_call(
        kernel,
        out_shape=outs,
        in_specs=[smem() if a.ndim == 1 else vmem() for a in args],
        out_specs=jax.tree.map(lambda _: vmem(), outs),
        scratch_shapes=[pltpu.VMEM(s, F32) for s in scratch],
        name=name,
    )(*args)


def onehot(idx, entries):
    spots = jnp.arange(3 * entries, dtype=jnp.int32) % entries
    return (idx.reshape(-1, 1) == spots).astype(BF16)


def make_shards(strips, tiles):
    few = strips <= 8 and strips & (strips - 1) == 0
    swap = [(0, 1), (1, 0)]

    def dest(row, d):
        return row ^ d if few else d

    def exchange(blocks, axis="rows"):
        if few:
            return [blocks[0]] + [
                lax.ppermute(blocks[d], axis, [(i, i ^ d) for i in range(strips)]) for d in range(1, strips)
            ]
        moved = lax.all_to_all(jnp.stack(blocks), axis, 0, 0)
        return [moved[d] for d in range(strips)]

    def across(v):
        return lax.ppermute(v, "chan", swap)

    def shards(features, gate, decay_idx, log_table, rate, proj_row, proj_col, conv_w, conv_b, d_skip):
        height, width, channels = features.shape
        entries, states = log_table.shape[0], rate.shape[0]
        strip = width // strips
        cells, total, count = height * width, strips * height, strip + 2
        skip, bias = d_skip.reshape(1, channels), conv_b.reshape(1, channels)

        rounds = [[(i, (i + d) % tiles) for i in range(tiles)] for d in range(1, tiles)]
        own = [features] + [lax.ppermute(features, "cols", pairs) for pairs in rounds]
        idx = [decay_idx] + [lax.ppermute(decay_idx, "cols", pairs) for pairs in rounds]
        other = [across(f) for f in own]
        proj_row2, proj_col2 = across(proj_row), across(proj_col)
        conv_w2, bias2 = across(conv_w), across(bias)
        hots = [onehot(i.T, entries) for i in idx]
        if few:
            whole = exchange([decay_idx] * strips)
            row = lax.axis_index("rows")
            order = jnp.arange(strips) ^ row
            parts = jnp.stack([w.reshape(height, strips, strip) for w in whole])
            mine = lax.dynamic_index_in_dim(parts, row, 2, keepdims=False)
            mine = sum(
                jnp.where((order == k)[:, None, None], mine[k][None], 0) for k in range(strips)
            )
        else:
            mine = lax.all_to_all(
                decay_idx.reshape(height, strips, strip).transpose(1, 0, 2), "rows", 0, 0
            )
        hot_strip = onehot(mine, entries)

        block = jax.ShapeDtypeStruct((count * height * 3 // 2, LANES), BF16)
        sent = call(
            lambda *r: row_kernel((tiles, strips, height, width, strip), dest, *r),
            [rate, *own, *other, *hots, log_table, proj_row, proj_row2, skip],
            [block] * strips,
            [(tiles * cells, LANES)] * 5 + [((width + 2) * height, LANES)] * 2,
            "rows",
        )
        got = exchange(sent)
        got2 = [across(b) for b in got]
        back = jax.ShapeDtypeStruct((height * strip * 3 // 2, LANES), BF16)
        pitch = total + 2 * SUB
        sent = call(
            lambda *r: column_kernel((strips, height, strip), dest, *r),
            [rate, *got, *got2, hot_strip, log_table, proj_col, proj_col2, conv_w, conv_w2, bias, bias2, skip],
            [back] * strips,
            [(count * pitch, LANES)] * 2 + [(total * strip, LANES)] * 7,
            "columns",
        )
        got = exchange(sent)
        return call(
            lambda *r: gate_kernel((strips, height, width, strip), dest, *r),
            [*got, gate],
            jax.ShapeDtypeStruct(features.shape, BF16),
            [(cells, LANES)] * 2,
            "gate",
        )

    return shards


def solution(mesh):
    placed = (
        P(("slides", "rows"), "cols", "chan"),
        P(("slides", "rows"), "cols", "chan"),
        P(("slides", "rows"), "cols"),
        P(None, "chan"),
        P(),
        P("chan", None),
        P("chan", None),
        P(None, None, "chan"),
        P("chan"),
        P("chan"),
    )
    return jax.shard_map(
        make_shards(mesh.shape["rows"], mesh.shape["cols"]),
        mesh=mesh,
        in_specs=placed,
        out_specs=P(("slides", "rows"), "cols", "chan"),
        check_vma=False,
    )
```

```python
import jax
import jax.numpy as jnp
from jax import lax
from jax.experimental import pallas as pl
from jax.experimental.pallas import tpu as pltpu
from jax.sharding import PartitionSpec as P


LANES = 128
SUB = 8
UNROLL = 4
LOG2E = 1.4426950408889634
F32 = jnp.float32
BF16 = jnp.bfloat16


def low_half(shape):
    return lax.broadcasted_iota(jnp.int32, shape, len(shape) - 1) < LANES // 2


def twice(v):
    return jnp.concatenate([v, v], axis=-1)


def split3(t):
    hi = t.astype(BF16)
    rest = t - hi.astype(F32)
    mid = rest.astype(BF16)
    low = (rest - mid.astype(F32)).astype(BF16)
    return jnp.concatenate([hi, mid, low], axis=0)


def tables(table_ref):
    t = table_ref[...] * LOG2E
    return split3(t[:, :LANES]), split3(twice(t[:, LANES:]))


def dot(a, b):
    return jnp.dot(a, b, preferred_element_type=F32)


def fill_rates(rate_ref, rates):
    half = low_half((SUB, LANES))
    states = rate_ref.shape[0]
    for s in range(states):
        rates[s * SUB : (s + 1) * SUB, :] = jnp.full((SUB, LANES), rate_ref[s], F32)
    for j in range(states // 2):
        at = (states + j) * SUB
        rates[at : at + SUB, :] = jnp.where(half, rate_ref[2 * j], rate_ref[2 * j + 1])


def steps(count, step, carry):
    first = count % UNROLL
    for i in range(first):
        carry = step(i, carry)

    def body(i, carry):
        for k in range(UNROLL):
            carry = step(first + i * UNROLL + k, carry)
        return carry

    return lax.fori_loop(0, count // UNROLL, body, carry)


def pitch_of(rows):
    return rows + SUB // 2 if rows % SUB == 0 else rows


def advance(carry, xa, xb, la, lb, drive, out, rates):
    states = rates.shape[0] // SUB * 2 // 3
    shape = xa.shape
    half = low_half(shape)
    drive = [drive(s) for s in range(states)]
    out = None if out is None else [out(s) for s in range(states)]
    new, ya, yb = [], [], []
    for s in range(states):
        st = jnp.exp2(la * rates[s * SUB : s * SUB + shape[0], :]) * carry[s] + drive[s] * xa
        new.append(st)
        if out:
            ya.append(out[s] * st)
    for j in range(states // 2):
        b = jnp.where(half, drive[2 * j], drive[2 * j + 1])
        at = (states + j) * SUB
        st = jnp.exp2(lb * rates[at : at + shape[0], :]) * carry[states + j] + b * xb
        new.append(st)
        if out:
            yb.append(jnp.where(half, out[2 * j], out[2 * j + 1]) * st)

    def tree(v):
        while len(v) > 1:
            v = [v[i] + v[i + 1] for i in range(0, len(v) - 1, 2)] + v[len(v) & ~1 :]
        return v[0] if v else None

    yb = tree(yb)
    return tuple(new), tree(ya), None if yb is None else yb + pltpu.roll(yb, LANES // 2, 1)


def spread(coeff, column):
    return jnp.broadcast_to(coeff[:, column : column + 1], (coeff.shape[0], LANES))


def spread_all(cf_ref, count, matrix, permute):
    for (column, to, rows), (column2, to2, rows2) in zip(matrix[::2], matrix[1::2]):
        v = cf_ref[:rows, : 3 * count]
        lane = lax.broadcasted_iota(jnp.int32, v.shape, 1)
        hi = v.astype(BF16).astype(F32)
        mid = (v - hi).astype(BF16).astype(F32)
        parts = jnp.where(lane < count, hi, jnp.where(lane < 2 * count, mid, v - hi - mid)).astype(BF16)
        shape = (3 * count, 2 * LANES)
        source = lax.broadcasted_iota(jnp.int32, shape, 0) % count
        wanted = jnp.where(lax.broadcasted_iota(jnp.int32, shape, 1) < LANES, column, column2)
        wide = dot(parts, (source == wanted).astype(BF16))
        to[...] = wide[:, :LANES]
        to2[...] = wide[:, LANES:]
    for column, to, rows in permute:
        to[...] = spread(cf_ref[:rows, :], column)


def thrice(v):
    return jnp.concatenate([v, v, v], axis=-1)


def row_kernel(dims, dest, *refs):
    tiles, strips, height, width, strip = dims
    rate_ref = refs[0]
    own, other = refs[1 : 1 + tiles], refs[1 + tiles : 1 + 2 * tiles]
    hots = refs[1 + 2 * tiles : 1 + 3 * tiles]
    table_ref, proj_ref, proj2_ref, skip_ref = refs[1 + 3 * tiles : 5 + 3 * tiles]
    outs = refs[5 + 3 * tiles : 5 + 3 * tiles + strips]
    scratch = refs[5 + 3 * tiles + strips :]
    raw, xa_ref, xb_ref, la_ref, lb_ref, cf_ref, drives, weights, ya_ref, yb_ref, rates = scratch[:3], *scratch[3:]
    states = rate_ref.shape[0]
    cells = height * width
    pitch = pitch_of(width)
    col = lax.axis_index("cols")
    row = lax.axis_index("rows")

    ta, tb = tables(table_ref)
    proj, proj2 = thrice(proj_ref[...]), thrice(proj2_ref[...])
    for d in range(tiles):
        x = own[d][...].reshape(cells, -1)
        part = pl.ds(d * cells, cells)
        coeff = dot(x, proj) + dot(other[d][...].reshape(cells, -1), proj2)
        xf = x.astype(F32)
        xa, xb = xf[:, :LANES], twice(xf[:, LANES:])
        if 0 < d < tiles - 1:
            there = (col >= d).astype(F32)
            xa, xb = xa * there, xb * there
        for h in range(height):
            to, cut = pl.ds((d * height + h) * pitch, width), slice(h * width, (h + 1) * width)
            raw[0][to, :] = xa[cut]
            raw[1][to, :] = xb[cut]
            raw[2][to, : 6 * states] = coeff[cut]
        hot = hots[d][...]
        la_ref[part, :] = dot(hot, ta)
        lb_ref[part, :] = dot(hot, tb)

    fill_rates(rate_ref, rates)
    for d in range(tiles):

        def order(w, unused, d=d):
            for g in range(height // SUB):
                place = pl.ds((d * height + g * SUB) * pitch + w, SUB, stride=pitch)
                to = pl.ds(pl.multiple_of(d * cells + w * height + g * SUB, SUB), SUB)
                for old, new in zip(raw, (xa_ref, xb_ref, cf_ref)):
                    new[to, :] = old[place, :]
            return unused

        steps(width, order, 0)
    size = tiles * cells
    every = [(s, drives.at[s * size : (s + 1) * size, :], size) for s in range(states)]
    every += [(states + s, weights.at[s * cells : (s + 1) * cells, :], cells) for s in range(states)]
    cut = states * 7 // 8 // 2 * 2
    spread_all(cf_ref, 2 * states, every[:cut], every[cut:])

    skip = skip_ref[...]
    skip_a, skip_b = skip[:, :LANES], twice(skip[:, LANES:])
    last_left = (col >= tiles - 1).astype(F32)

    for g in range(height // SUB):

        def step(carry, d, w, wanted, g=g):
            here = w * height + g * SUB
            at = pl.ds(pl.multiple_of(d * cells + here, SUB), SUB)
            xa, xb = xa_ref[at, :], xb_ref[at, :]

            def drive(s):
                return drives[pl.ds(pl.multiple_of((s * tiles + d) * cells + here, SUB), SUB), :]

            def out(s):
                if d:
                    return spread(cf_ref[at, :], states + s)
                return weights[pl.ds(pl.multiple_of(s * cells + here, SUB), SUB), :]

            carry, ya, yb = advance(
                carry, xa, xb, la_ref[at, :], lb_ref[at, :], drive, out if wanted else None, rates
            )
            if wanted:
                ya, yb = ya + skip_a * xa, yb + skip_b * xb
            return carry, ya, yb

        def put(c, ya, yb, g=g):
            at = pl.ds(pl.multiple_of(c * height + g * SUB, SUB), SUB)
            ya_ref[at, :] = ya
            yb_ref[at, :] = yb

        carry = tuple(jnp.zeros((SUB, LANES), F32) for _ in range(states + states // 2))
        for d in range(tiles - 1, 0, -1):
            carry = steps(width - (d == 1), lambda w, s, d=d: step(s, d, w, False)[0], carry)
            if d == tiles - 1:
                carry = tuple(v * last_left for v in carry)
        carry, ya, yb = step(carry, 1, width - 1, True)
        if tiles == 2:
            carry = tuple(v * last_left for v in carry)
            ya, yb = ya * last_left, yb * last_left
        put(0, ya, yb)

        def body(w, s):
            s, ya, yb = step(s, 0, w, True)
            put(w + 1, ya, yb)
            return s

        carry = steps(width, body, carry)
        _, ya, yb = step(carry, tiles - 1, 0, True)
        inside = 1.0 - last_left
        put(width + 1, ya * inside, yb * inside)

    count = strip + 2
    for d in range(strips):
        start = pl.multiple_of(dest(row, d) * strip * height, SUB)
        from_ = pl.ds(start, count * height)
        outs[d][: count * height, :] = ya_ref[from_, :].astype(BF16)
        yb = yb_ref[from_, :].reshape(count, 2, height // 2, LANES)
        low, high = yb[:, 0], yb[:, 1]
        packed = jnp.where(low_half(low.shape), low, high).reshape(count * height // 2, LANES)
        outs[d][count * height :, :] = packed.astype(BF16)


def unpack(v):
    half = low_half(v.shape)
    turned = pltpu.roll(v, LANES // 2, 1)
    return jnp.where(half, v, turned), jnp.where(half, turned, v)


def column_kernel(dims, dest, *refs):
    strips, height, strip = dims
    rate_ref = refs[0]
    blocks = (refs[1 : 1 + strips], refs[1 + strips : 1 + 2 * strips])
    at = 1 + 2 * strips
    hot_ref, table_ref = refs[at : at + 2]
    projs = refs[at + 2 : at + 4]
    conv_ws = refs[at + 4 : at + 6]
    conv_bs = refs[at + 6 : at + 8]
    skip_ref = refs[at + 8]
    outs = refs[at + 9 : at + 9 + strips]
    scratch = refs[at + 9 + strips :]
    ra_ref, rb_ref, raw = *scratch[:2], scratch[2:5]
    xa_ref, xb_ref, cf_ref, la_ref, lb_ref, ya_ref, yb_ref, drives, weights, rates = scratch[5:]
    states = rate_ref.shape[0]
    row = lax.axis_index("rows")
    total = strips * height
    pitch = total + 2 * SUB
    leap = pitch_of(total)
    count = strip + 2
    fill_rates(rate_ref, rates)

    ta, tb = tables(table_ref)
    hot = hot_ref[...]
    la_ref[...] = dot(hot, ta)
    lb_ref[...] = dot(hot, tb)
    zero = jnp.zeros((SUB, LANES), F32)
    for k in range(count):
        for ref in (ra_ref, rb_ref):
            ref[pl.ds(k * pitch, SUB), :] = zero
            ref[pl.ds(k * pitch + SUB + total, SUB), :] = zero

    for side in (1, 0):
        for d in range(strips):
            base = pl.multiple_of(dest(row, d) * height, SUB) + SUB
            va = blocks[side][d][: count * height, :].astype(F32)
            low, high = unpack(blocks[side][d][count * height :, :].astype(F32))
            h2 = height // 2
            for k in range(count):
                to = pl.multiple_of(base + k * pitch, SUB)
                ra_ref[pl.ds(to, height), :] = va[k * height : (k + 1) * height]
                rb_ref[pl.ds(to, h2), :] = low[k * h2 : (k + 1) * h2]
                rb_ref[pl.ds(pl.multiple_of(to + h2, SUB), h2), :] = high[k * h2 : (k + 1) * h2]
        taps = conv_ws[side][...]
        bias = conv_bs[side][...]
        for src, dst, cut in (
            (ra_ref, raw[0], lambda v: v[..., :LANES]),
            (rb_ref, raw[1], lambda v: twice(v[..., LANES:])),
        ):
            cut_taps, add = cut(taps), cut(bias)
            taps_wide = [[jnp.broadcast_to(cut_taps[a, b][None, :], (SUB, LANES)) for b in range(3)] for a in range(3)]
            start = jnp.broadcast_to(add, (SUB, LANES))

            def conv(i, unused, src=src, dst=dst, taps_wide=taps_wide, start=start):
                sums = [start] * strip
                for k in range(count):
                    for a in range(3):
                        v = src[pl.ds(k * pitch + i * SUB + SUB - 1 + a, SUB), :]
                        for b in range(3):
                            if 0 <= k - b < strip:
                                sums[k - b] = sums[k - b] + taps_wide[a][b] * v
                for k in range(strip):
                    v = sums[k] / (1.0 + jnp.exp(-sums[k]))
                    dst[pl.ds(k * leap + i * SUB, SUB), :] = v.astype(BF16).astype(F32)
                return unused

            lax.fori_loop(0, total // SUB, conv, 0)
        proj = thrice(projs[side][...])
        for k in range(strip):
            at = pl.ds(k * leap, total)
            part = dot(raw[0][at, :].astype(BF16), proj[:LANES]) + dot(
                raw[1][at, : LANES // 2].astype(BF16), proj[LANES:]
            )
            raw[2][at, : 6 * states] = part if side else part + raw[2][at, : 6 * states]

    skip = skip_ref[...]
    skip_a, skip_b = skip[:, :LANES], twice(skip[:, LANES:])

    def here(h, base=0):
        at = base + h * strip
        return pl.ds(at if strip % SUB else pl.multiple_of(at, SUB), strip)

    def order(h, unused):
        for old, new in zip(raw, (xa_ref, xb_ref, cf_ref)):
            new[here(h), :] = old[pl.ds(h, strip, stride=leap), :]
        return unused

    steps(total, order, 0)
    cells = total * strip
    every = [(s, drives.at[s * cells : (s + 1) * cells, :], cells) for s in range(states)]
    every += [(states + s, weights.at[s * cells : (s + 1) * cells, :], cells) for s in range(states)]
    cut = states * 5 // 4 // 2 * 2
    spread_all(cf_ref, 2 * states, every[:cut], every[cut:])

    def body(h, carry):
        at = here(h)
        xa, xb = xa_ref[at, :], xb_ref[at, :]
        carry, ya, yb = advance(
            carry,
            xa,
            xb,
            la_ref[at, :],
            lb_ref[at, :],
            lambda s: drives[here(h, s * cells), :],
            lambda s: weights[here(h, s * cells), :],
            rates,
        )
        ya_ref[at, :] = ya + skip_a * xa
        yb_ref[at, :] = yb + skip_b * xb
        return carry

    zeros = tuple(jnp.zeros((strip, LANES), F32) for _ in range(states + states // 2))
    steps(total, body, zeros)

    cells = height * strip
    for d in range(strips):
        start = pl.multiple_of(dest(row, d) * cells, SUB)
        from_ = pl.ds(start, cells)
        outs[d][:cells, :] = ya_ref[from_, :].astype(BF16)
        yb = yb_ref[from_, :]
        low, high = yb[: cells // 2], yb[cells // 2 :]
        outs[d][cells:, :] = jnp.where(low_half(low.shape), low, high).astype(BF16)


def gate_kernel(dims, dest, *refs):
    strips, height, width, strip = dims
    blocks, gate_ref, out_ref, ya_ref, yb_ref = refs[:strips], *refs[strips:]
    row = lax.axis_index("rows")
    cells = height * strip
    for d in range(strips):
        va = blocks[d][:cells, :].astype(F32)
        low, high = unpack(blocks[d][cells:, :].astype(F32))
        left = dest(row, d) * strip
        for h in range(height):
            to = left + h * width
            to = pl.ds(to if strip % SUB else pl.multiple_of(to, SUB), strip)
            ya_ref[to, :] = va[h * strip : (h + 1) * strip]
            b, i = (low, h) if h < height // 2 else (high, h - height // 2)
            yb_ref[to, :] = b[i * strip : (i + 1) * strip]
    gate = gate_ref[...].astype(F32)
    gate = gate / (1.0 + jnp.exp(-gate))
    out_ref[:, :, :LANES] = (ya_ref[...].reshape(height, width, LANES) * gate[:, :, :LANES]).astype(BF16)
    yb = yb_ref[...].reshape(height, width, LANES)[:, :, : LANES // 2]
    out_ref[:, :, LANES:] = (yb * gate[:, :, LANES:]).astype(BF16)


def smem():
    return pl.BlockSpec(memory_space=pltpu.SMEM)


def vmem():
    return pl.BlockSpec(memory_space=pltpu.VMEM)


def call(kernel, args, outs, scratch):
    return pl.pallas_call(
        kernel,
        out_shape=outs,
        in_specs=[smem() if a.ndim == 1 else vmem() for a in args],
        out_specs=jax.tree.map(lambda _: vmem(), outs),
        scratch_shapes=[pltpu.VMEM(s, F32) for s in scratch],
    )(*args)


def onehot(idx, entries):
    spots = jnp.arange(3 * entries, dtype=jnp.int32) % entries
    return (idx.reshape(-1, 1) == spots).astype(BF16)


def make_shards(strips, tiles):
    few = strips <= 8 and strips & (strips - 1) == 0
    swap = [(0, 1), (1, 0)]

    def dest(row, d):
        return row ^ d if few else d

    def exchange(blocks, axis="rows"):
        if few:
            return [blocks[0]] + [
                lax.ppermute(blocks[d], axis, [(i, i ^ d) for i in range(strips)]) for d in range(1, strips)
            ]
        moved = lax.all_to_all(jnp.stack(blocks), axis, 0, 0)
        return [moved[d] for d in range(strips)]

    def across(v):
        return lax.ppermute(v, "chan", swap)

    def shards(features, gate, decay_idx, log_table, rate, proj_row, proj_col, conv_w, conv_b, d_skip):
        height, width, channels = features.shape
        entries, states = log_table.shape[0], rate.shape[0]
        strip = width // strips
        cells, total, count = height * width, strips * height, strip + 2
        skip, bias = d_skip.reshape(1, channels), conv_b.reshape(1, channels)

        rounds = [[(i, (i + d) % tiles) for i in range(tiles)] for d in range(1, tiles)]
        own = [features] + [lax.ppermute(features, "cols", pairs) for pairs in rounds]
        idx = [decay_idx] + [lax.ppermute(decay_idx, "cols", pairs) for pairs in rounds]
        other = [across(features)]
        other += [across(f) for f in own[1:]]
        proj_row2, proj_col2 = across(proj_row), across(proj_col)
        conv_w2, bias2 = across(conv_w), across(bias)
        hots = [onehot(i.T, entries) for i in idx]
        if few:
            whole = exchange([decay_idx] * strips)
            row = lax.axis_index("rows")
            order = jnp.arange(strips) ^ row
            parts = jnp.stack([w.reshape(height, strips, strip) for w in whole])
            mine = lax.dynamic_index_in_dim(parts, row, 2, keepdims=False)
            mine = sum(
                jnp.where((order == k)[:, None, None], mine[k][None], 0) for k in range(strips)
            )
        else:
            mine = lax.all_to_all(
                decay_idx.reshape(height, strips, strip).transpose(1, 0, 2), "rows", 0, 0
            )
        hot_strip = onehot(mine, entries)

        block = jax.ShapeDtypeStruct((count * height * 3 // 2, LANES), BF16)
        sent = call(
            lambda *r: row_kernel((tiles, strips, height, width, strip), dest, *r),
            [rate, *own, *other, *hots, log_table, proj_row, proj_row2, skip],
            [block] * strips,
            [(tiles * height * pitch_of(width), LANES)] * 3
            + [(tiles * cells, LANES)] * 5
            + [(states * tiles * cells, LANES), (states * cells, LANES)]
            + [((width + 2) * height, LANES)] * 2
            + [(states * 3 // 2 * SUB, LANES)],
        )
        got = exchange(sent)
        got2 = [across(b) for b in got]
        back = jax.ShapeDtypeStruct((height * strip * 3 // 2, LANES), BF16)
        pitch = total + 2 * SUB
        sent = call(
            lambda *r: column_kernel((strips, height, strip), dest, *r),
            [rate, *got, *got2, hot_strip, log_table, proj_col, proj_col2, conv_w, conv_w2, bias, bias2, skip],
            [back] * strips,
            [(count * pitch, LANES)] * 2
            + [(strip * pitch_of(total), LANES)] * 3
            + [(total * strip, LANES)] * 7
            + [(states * total * strip, LANES)] * 2
            + [(states * 3 // 2 * SUB, LANES)],
        )
        got = exchange(sent)
        return call(
            lambda *r: gate_kernel((strips, height, width, strip), dest, *r),
            [*got, gate],
            jax.ShapeDtypeStruct(features.shape, BF16),
            [(cells, LANES)] * 2,
        )

    return shards


def solution(mesh):
    placed = (
        P(("slides", "rows"), "cols", "chan"),
        P(("slides", "rows"), "cols", "chan"),
        P(("slides", "rows"), "cols"),
        P(None, "chan"),
        P(),
        P("chan", None),
        P("chan", None),
        P(None, None, "chan"),
        P("chan"),
        P("chan"),
    )
    shards = make_shards(mesh.shape["rows"], mesh.shape["cols"])

    return jax.shard_map(
        shards, mesh=mesh, in_specs=placed, out_specs=P(("slides", "rows"), "cols", "chan"), check_vma=False
    )
```

```python
import jax
import jax.numpy as jnp
from jax import lax
from jax.experimental import pallas as pl
from jax.experimental.pallas import tpu as pltpu
from jax.sharding import PartitionSpec as P


LANES = 128
SUB = 8
UNROLL = 4
LOG2E = 1.4426950408889634
F32 = jnp.float32
BF16 = jnp.bfloat16


def low_half(shape):
    return lax.broadcasted_iota(jnp.int32, shape, len(shape) - 1) < LANES // 2


def twice(v):
    return jnp.concatenate([v, v], axis=-1)


def split3(t):
    hi = t.astype(BF16)
    rest = t - hi.astype(F32)
    mid = rest.astype(BF16)
    low = (rest - mid.astype(F32)).astype(BF16)
    return jnp.concatenate([hi, mid, low], axis=0)


def tables(table_ref):
    t = table_ref[...] * LOG2E
    return split3(jnp.concatenate([t[:, :LANES], twice(t[:, LANES:])], axis=-1))


def mark(entry, entries):
    lane = lax.broadcasted_iota(jnp.int32, entry.shape, 1)
    spot = jnp.where(lane < 3 * entries, lane % entries, -1).astype(F32)
    return (entry == spot).astype(F32).astype(BF16)


def dot(a, b):
    return jnp.dot(a, b, preferred_element_type=F32)


def dot_t(a, b):
    return lax.dot_general(a, b, (((1,), (1,)), ((), ())), preferred_element_type=F32)


def fill_rates(rate_ref, rates):
    half = low_half((SUB, LANES))
    states = rate_ref.shape[0]
    for s in range(states):
        rates[s * SUB : (s + 1) * SUB, :] = jnp.full((SUB, LANES), rate_ref[s], F32)
    for j in range(states // 2):
        at = (states + j) * SUB
        rates[at : at + SUB, :] = jnp.where(half, rate_ref[2 * j], rate_ref[2 * j + 1])


def steps(count, step, carry):
    first = count % UNROLL
    for i in range(first):
        carry = step(i, carry)

    def body(i, carry):
        for k in range(UNROLL):
            carry = step(first + i * UNROLL + k, carry)
        return carry

    return lax.fori_loop(0, count // UNROLL, body, carry)


def pitch_of(rows):
    return rows + SUB // 2 if rows % SUB == 0 else rows


def advance(carry, xa, xb, la, lb, drive, out, rates):
    states = rates.shape[0] // SUB * 2 // 3
    shape = xa.shape
    half = low_half(shape)
    drive = [drive(s) for s in range(states)]
    out = None if out is None else [out(s) for s in range(states)]
    new, ya, yb = [], [], []
    for s in range(states):
        st = jnp.exp2(la * rates[s * SUB : s * SUB + shape[0], :]) * carry[s] + drive[s] * xa
        new.append(st)
        if out:
            ya.append(out[s] * st)
    for j in range(states // 2):
        b = jnp.where(half, drive[2 * j], drive[2 * j + 1])
        at = (states + j) * SUB
        st = jnp.exp2(lb * rates[at : at + shape[0], :]) * carry[states + j] + b * xb
        new.append(st)
        if out:
            yb.append(jnp.where(half, out[2 * j], out[2 * j + 1]) * st)

    def tree(v):
        while len(v) > 1:
            v = [v[i] + v[i + 1] for i in range(0, len(v) - 1, 2)] + v[len(v) & ~1 :]
        return v[0] if v else None

    yb = tree(yb)
    return tuple(new), tree(ya), None if yb is None else yb + pltpu.roll(yb, LANES // 2, 1)


def spread(coeff, column):
    return jnp.broadcast_to(coeff[:, column : column + 1], (coeff.shape[0], LANES))


def thirds(v, count):
    lane = lax.broadcasted_iota(jnp.int32, v.shape, 1)
    hi = v.astype(BF16).astype(F32)
    mid = (v - hi).astype(BF16).astype(F32)
    return jnp.where(lane < count, hi, jnp.where(lane < 2 * count, mid, v - hi - mid))


def spread_all(cf_ref, count, matrix, permute):
    for (column, to, rows), (column2, to2, rows2) in zip(matrix[::2], matrix[1::2]):
        parts = thirds(cf_ref[:rows, : 3 * count], count).astype(BF16)
        shape = (3 * count, 2 * LANES)
        source = lax.broadcasted_iota(jnp.int32, shape, 0) % count
        wanted = jnp.where(lax.broadcasted_iota(jnp.int32, shape, 1) < LANES, column, column2)
        wide = dot(parts, (source == wanted).astype(BF16))
        to[...] = wide[:, :LANES]
        to2[...] = wide[:, LANES:]
    for column, to, rows in permute:
        to[...] = spread(cf_ref[:rows, :], column)


def thrice(v):
    return jnp.concatenate([v, v, v], axis=0)


def row_kernel(dims, dest, *refs):
    tiles, strips, height, width, strip = dims
    rate_ref = refs[0]
    own, other = refs[1 : 1 + tiles], refs[1 + tiles : 1 + 2 * tiles]
    idxs = refs[1 + 2 * tiles : 1 + 3 * tiles]
    table_ref, proj_ref, proj2_ref, skip_ref = refs[1 + 3 * tiles : 5 + 3 * tiles]
    outs = refs[5 + 3 * tiles : 5 + 3 * tiles + strips]
    scratch = refs[5 + 3 * tiles + strips :]
    raw, xa_ref, xb_ref, la_ref, lb_ref, cf_ref, drives, weights, ya_ref, yb_ref, rates = scratch[:3], *scratch[3:13]
    entry_ref, hot_ref = scratch[13:]
    states = rate_ref.shape[0]
    cells = height * width
    pitch = pitch_of(width)
    col = lax.axis_index("cols")
    row = lax.axis_index("rows")

    table = tables(table_ref)
    entries = table_ref.shape[0]
    entry_ref[...] = jnp.zeros(entry_ref.shape, F32)
    proj, proj2 = thrice(proj_ref[...]), thrice(proj2_ref[...])
    for d in range(tiles):
        x = own[d][...].reshape(cells, -1)
        part = pl.ds(d * cells, cells)
        coeff = dot_t(x, proj) + dot_t(other[d][...].reshape(cells, -1), proj2)
        xf = x.astype(F32)
        xa, xb = xf[:, :LANES], twice(xf[:, LANES:])
        if 0 < d < tiles - 1:
            there = (col >= d).astype(F32)
            xa, xb = xa * there, xb * there
        for h in range(height):
            to, cut = pl.ds((d * height + h) * pitch, width), slice(h * width, (h + 1) * width)
            raw[0][to, :] = xa[cut]
            raw[1][to, :] = xb[cut]
            raw[2][to, : 6 * states] = coeff[cut]
        entry = idxs[d][...].astype(F32)
        if d == 0:
            entry_ref[:, :width] = entry
        for w in range(width):
            hot_ref[w * height : (w + 1) * height, :] = mark(spread(entry, w), entries)
        logs = dot(hot_ref[:, : 3 * entries], table)
        la_ref[part, :] = logs[:, :LANES]
        lb_ref[part, :] = logs[:, LANES:]

    fill_rates(rate_ref, rates)
    for d in range(tiles):

        def order(w, unused, d=d):
            for g in range(height // SUB):
                place = pl.ds((d * height + g * SUB) * pitch + w, SUB, stride=pitch)
                to = pl.ds(pl.multiple_of(d * cells + w * height + g * SUB, SUB), SUB)
                for old, new in zip(raw, (xa_ref, xb_ref, cf_ref)):
                    new[to, :] = old[place, :]
            return unused

        steps(width, order, 0)
    size = tiles * cells
    every = [(s, drives.at[s * size : (s + 1) * size, :], size) for s in range(states)]
    every += [(states + s, weights.at[s * cells : (s + 1) * cells, :], cells) for s in range(states)]
    cut = states * 7 // 8 // 2 * 2
    spread_all(cf_ref, 2 * states, every[:cut], every[cut:])

    skip = skip_ref[...]
    skip_a, skip_b = skip[:, :LANES], twice(skip[:, LANES:])
    last_left = (col >= tiles - 1).astype(F32)

    for g in range(height // SUB):

        def step(carry, d, w, wanted, g=g):
            here = w * height + g * SUB
            at = pl.ds(pl.multiple_of(d * cells + here, SUB), SUB)
            xa, xb = xa_ref[at, :], xb_ref[at, :]

            def drive(s):
                return drives[pl.ds(pl.multiple_of((s * tiles + d) * cells + here, SUB), SUB), :]

            def out(s):
                if d:
                    return spread(cf_ref[at, :], states + s)
                return weights[pl.ds(pl.multiple_of(s * cells + here, SUB), SUB), :]

            carry, ya, yb = advance(
                carry, xa, xb, la_ref[at, :], lb_ref[at, :], drive, out if wanted else None, rates
            )
            if wanted:
                ya, yb = ya + skip_a * xa, yb + skip_b * xb
            return carry, ya, yb

        def put(c, ya, yb, g=g):
            at = pl.ds(pl.multiple_of(c * height + g * SUB, SUB), SUB)
            ya_ref[at, :] = ya
            yb_ref[at, :] = yb

        carry = tuple(jnp.zeros((SUB, LANES), F32) for _ in range(states + states // 2))
        for d in range(tiles - 1, 0, -1):
            carry = steps(width - (d == 1), lambda w, s, d=d: step(s, d, w, False)[0], carry)
            if d == tiles - 1:
                carry = tuple(v * last_left for v in carry)
        carry, ya, yb = step(carry, 1, width - 1, True)
        if tiles == 2:
            carry = tuple(v * last_left for v in carry)
            ya, yb = ya * last_left, yb * last_left
        put(0, ya, yb)

        def body(w, s):
            s, ya, yb = step(s, 0, w, True)
            put(w + 1, ya, yb)
            return s

        carry = steps(width, body, carry)
        _, ya, yb = step(carry, tiles - 1, 0, True)
        inside = 1.0 - last_left
        put(width + 1, ya * inside, yb * inside)

    pack_blocks(outs, dest, row, strip, height, ya_ref, yb_ref, entry_ref)


def pack_blocks(outs, dest, row, strip, height, ya_ref, yb_ref, entry_ref):
    count = strip + 2
    rows = count * height * 3 // 2
    for d in range(len(outs)):
        start = pl.multiple_of(dest(row, d) * strip * height, SUB)
        from_ = pl.ds(start, count * height)
        outs[d][: count * height, :] = ya_ref[from_, :].astype(BF16)
        yb = yb_ref[from_, :].reshape(count, 2, height // 2, LANES)
        low, high = yb[:, 0], yb[:, 1]
        packed = jnp.where(low_half(low.shape), low, high).reshape(count * height // 2, LANES)
        outs[d][count * height : rows, :] = packed.astype(BF16)
        entry = pltpu.roll(entry_ref[...], LANES - dest(row, d) * strip, 1)
        outs[d][rows:, :] = entry.astype(BF16)


def split2(v):
    hi = v.astype(BF16).astype(F32)
    return hi, v - hi


def own_kernel(dims, *refs):
    height, width = dims
    inputs, (xa_ref, xb_ref, la_ref, lb_ref, cf_ref, rates, skips, entry_ref, marks) = refs[:6], refs[6:15]
    raw, hot_ref, held, arrived = refs[15:18], refs[18], refs[19:25], refs[25]
    copies = [pltpu.make_async_copy(a, b, arrived.at[i]) for i, (a, b) in enumerate(zip(inputs, held))]
    for copy in copies:
        copy.start()
    for copy in copies:
        copy.wait()
    rate_ref, own_ref, idx_ref, table_ref, proj_ref, skip_ref = held
    states = rate_ref.shape[0]
    cells = height * width
    pitch = pitch_of(width)

    table = tables(table_ref)
    marks[...] = table
    entries = table_ref.shape[0]
    x = own_ref[...].reshape(cells, -1)
    coeff = dot_t(x, thrice(proj_ref[...]))
    xf = x.astype(F32)
    xa, xb = xf[:, :LANES], twice(xf[:, LANES:])
    for h in range(height):
        to, cut = pl.ds(h * pitch, width), slice(h * width, (h + 1) * width)
        raw[0][to, :] = xa[cut]
        raw[1][to, :] = xb[cut]
        raw[2][to, : 6 * states] = coeff[cut]
    entry = idx_ref[...].astype(F32)
    entry_ref[...] = jnp.zeros(entry_ref.shape, F32)
    entry_ref[:, :width] = entry
    for w in range(width):
        hot_ref[w * height : (w + 1) * height, :] = mark(spread(entry, w), entries)
    logs = dot(hot_ref[:, : 3 * entries], table)
    la_ref[...] = logs[:, :LANES]
    lb_ref[...] = logs[:, LANES:]
    fill_rates(rate_ref, rates)
    skip = skip_ref[...]
    skips[:SUB, :] = jnp.broadcast_to(skip[:, :LANES], (SUB, LANES))
    skips[SUB:, :] = jnp.broadcast_to(twice(skip[:, LANES:]), (SUB, LANES))
    in_order(dims, raw, (xa_ref, xb_ref, cf_ref))


def in_order(dims, olds, news, add=None):
    height, width = dims
    pitch = pitch_of(width)

    def order(w, unused):
        for g in range(height // SUB):
            place = pl.ds(g * SUB * pitch + w, SUB, stride=pitch)
            to = pl.ds(pl.multiple_of(w * height + g * SUB, SUB), SUB)
            for old, new in zip(olds, news):
                new[to, :] = old[place, :] if add is None else old[place, :] + add[to, :]
        return unused

    steps(width, order, 0)


def add_up(v):
    while len(v) > 1:
        v = [v[i] + v[i + 1] for i in range(0, len(v) - 1, 2)] + v[len(v) & ~1 :]
    return v[0]


def at_step(ref, i, cells, here):
    return ref[pl.ds(pl.multiple_of(i * cells + here, SUB), SUB), :]


def tile_kernel(dims, *refs):
    height, width = dims
    other_ref, proj2_ref, xa_ref, xb_ref, la_ref, lb_ref, half_ref, rates, skips, entry_ref = refs[:10]
    note_ref, ya_ref, yb_ref, sa_ref, sb_ref, cf_ref = refs[10:16]
    raw, drives, weights = refs[16:]
    kinds = rates.shape[0] // SUB
    states = kinds * 2 // 3
    cells = height * width
    pitch = pitch_of(width)

    coeff = dot_t(other_ref[...].reshape(cells, -1), thrice(proj2_ref[...]))
    for h in range(height):
        raw[h * pitch : h * pitch + width, : 6 * states] = coeff[h * width : (h + 1) * width]
    in_order(dims, (raw,), (cf_ref,), half_ref)
    every = [(s, drives.at[s * cells : (s + 1) * cells, :], cells) for s in range(states)]
    every += [(states + s, weights.at[s * cells : (s + 1) * cells, :], cells) for s in range(states)]
    cut = states * 5 // 4 // 2 * 2
    spread_all(cf_ref, 2 * states, every[:cut], every[cut:])

    skip_a, skip_b = skips[:SUB, :], skips[SUB:, :]
    for g in range(height // SUB):

        def step(w, carry, g=g):
            carry, sum_a, sum_b = carry
            here = w * height + g * SUB
            at = pl.ds(pl.multiple_of(here, SUB), SUB)
            xa, xb, la, lb = xa_ref[at, :], xb_ref[at, :], la_ref[at, :], lb_ref[at, :]
            carry, ya, yb = advance(
                carry,
                xa,
                xb,
                la,
                lb,
                lambda s: at_step(drives, s, cells, here),
                lambda s: at_step(weights, s, cells, here),
                rates,
            )
            sum_a, sum_b = sum_a + la, sum_b + lb
            ya_ref[at, :] = ya + skip_a * xa
            yb_ref[at, :] = yb + skip_b * xb
            sa_ref[at, :] = sum_a
            sb_ref[at, :] = sum_b
            return carry, sum_a, sum_b

        zero = jnp.zeros((SUB, LANES), F32)
        carry, _, _ = steps(width, step, ((zero,) * kinds, zero, zero))
        for i in range(0, kinds, 2):
            at = (g * kinds + i) * SUB
            note_ref[at : at + 2 * SUB, :] = jnp.concatenate(carry[i : i + 2], axis=0).astype(BF16)

    lane = lax.broadcasted_iota(jnp.int32, (height, LANES), 1)
    first = jnp.where(lane < 6 * states, thirds(cf_ref[:height, :], 2 * states), 0.0)
    a, a2 = split2(ya_ref[:height, :])
    b, b2 = split2(yb_ref[:height, :])
    extra = [
        jnp.where(lane == 6 * states, spread(entry_ref[...], 0), first),
        a,
        a2,
        jnp.where(low_half(b.shape), b, b2),
        ya_ref[cells - height :, :],
        yb_ref[cells - height :, :],
    ]
    for i, v in enumerate(extra):
        at = kinds * height + i * height
        note_ref[at : at + height, :] = v.astype(BF16)


def weigh_kernel(*refs):
    cf_ref, sa_ref, sb_ref, rates, out_ref, weights = refs
    kinds = rates.shape[0] // SUB
    states = kinds * 2 // 3
    cells = cf_ref.shape[0]
    half = low_half((SUB, LANES))
    every = [(states + s, weights.at[s * cells : (s + 1) * cells, :], cells) for s in range(states)]
    cut = states * 5 // 8 // 2 * 2
    spread_all(cf_ref, 2 * states, every[:cut], every[cut:])

    def step(i, unused):
        here = i * SUB
        at = pl.ds(pl.multiple_of(here, SUB), SUB)
        sum_a, sum_b = sa_ref[at, :], sb_ref[at, :]
        wide = [at_step(weights, s, cells, here) for s in range(states)]
        for k in range(kinds):
            j = k - states
            log, weight = (sum_a, wide[k]) if j < 0 else (sum_b, jnp.where(half, wide[2 * j], wide[2 * j + 1]))
            to = pl.ds(pl.multiple_of(k * cells + here, SUB), SUB)
            out_ref[to, :] = weight * jnp.exp2(log * rates[k * SUB : (k + 1) * SUB, :])
        return unused

    steps(cells // SUB, step, 0)


def join_kernel(dims, dest, *refs):
    strips, height, width, strip = dims
    own_ref, came_ref, ta_ref, tb_ref, brings, entry_ref, marks, rates = refs[:8]
    outs = refs[8 : 8 + strips]
    ya_ref, yb_ref = refs[8 + strips :]
    kinds = rates.shape[0] // SUB
    states = kinds * 2 // 3
    cells = height * width
    row = lax.axis_index("rows")
    right = (lax.axis_index("cols") == 1).astype(F32)
    half = low_half((SUB, LANES))

    def extra(i):
        at = (kinds + i) * height
        return came_ref[at : at + height, :].astype(F32)

    first = extra(0)
    log = dot(mark(spread(first, 6 * states), marks.shape[0] // 3)[:, : marks.shape[0]], marks[...])
    group = 2 * states
    coeff = first + pltpu.roll(first, LANES - group, 1) + pltpu.roll(first, LANES - 2 * group, 1)
    near_b = extra(3)
    near_b = near_b + pltpu.roll(near_b, LANES // 2, 1)
    near_a = extra(1) + extra(2)
    ya_ref[:height, :] = extra(4) * right
    yb_ref[:height, :] = extra(5) * right

    for g in range(height // SUB):

        def inflow(ref, scale, g=g):
            new = []
            for i in range(0, kinds, 2):
                at = (g * kinds + i) * SUB
                v = ref[at : at + 2 * SUB, :].astype(F32) * scale
                new += [v[:SUB], v[SUB:]]
            return tuple(new)

        def step(w, state, g=g):
            here = w * height + g * SUB
            at = pl.ds(pl.multiple_of(here, SUB), SUB)
            to = pl.ds(pl.multiple_of(here + height, SUB), SUB)
            terms = [at_step(brings, k, cells, here) * state[k] for k in range(kinds)]
            b = add_up(terms[states:])
            ya_ref[to, :] = ta_ref[at, :] + add_up(terms[:states])
            yb_ref[to, :] = tb_ref[at, :] + b + pltpu.roll(b, LANES // 2, 1)
            return state

        steps(width, step, inflow(came_ref, right))
        cut = slice(g * SUB, (g + 1) * SUB)
        state = inflow(own_ref, 1.0)
        wide = [spread(coeff[cut], states + s) for s in range(states)]
        wide += [jnp.where(half, wide[2 * j], wide[2 * j + 1]) for j in range(states // 2)]
        terms = []
        for k in range(kinds):
            part = log[cut, :LANES] if k < states else log[cut, LANES:]
            terms.append(wide[k] * (jnp.exp2(part * rates[k * SUB : (k + 1) * SUB, :]) * state[k]))
        b = add_up(terms[states:])
        at = slice((width + 1) * height + g * SUB, (width + 1) * height + (g + 1) * SUB)
        ya_ref[at, :] = (near_a[cut] + add_up(terms[:states])) * (1.0 - right)
        yb_ref[at, :] = (near_b[cut] + b + pltpu.roll(b, LANES // 2, 1)) * (1.0 - right)

    pack_blocks(outs, dest, row, strip, height, ya_ref, yb_ref, entry_ref)


def unpack(v):
    half = low_half(v.shape)
    turned = pltpu.roll(v, LANES // 2, 1)
    return jnp.where(half, v, turned), jnp.where(half, turned, v)


def column_kernel(dims, dest, *refs):
    strips, height, strip = dims
    rate_ref = refs[0]
    blocks = (refs[1 : 1 + strips], refs[1 + strips : 1 + 2 * strips])
    at = 1 + 2 * strips
    table_ref = refs[at]
    projs = refs[at + 1 : at + 3]
    conv_ws = refs[at + 3 : at + 5]
    conv_bs = refs[at + 5 : at + 7]
    skip_ref = refs[at + 7]
    outs = refs[at + 8 : at + 8 + strips]
    scratch = refs[at + 8 + strips :]
    ra_ref, rb_ref, raw = *scratch[:2], scratch[2:7]
    xa_ref, xb_ref, cf_ref, la_ref, lb_ref, ya_ref, yb_ref, drives, weights, rates, hot_ref = scratch[7:]
    states = rate_ref.shape[0]
    row = lax.axis_index("rows")
    total = strips * height
    pitch = total + 2 * SUB
    leap = pitch_of(total)
    count = strip + 2
    fill_rates(rate_ref, rates)

    table = tables(table_ref)
    entries = table_ref.shape[0]
    rows = count * height * 3 // 2
    for d in range(strips):
        entry = blocks[0][d][rows:, :].astype(F32)
        base = pl.multiple_of(dest(row, d) * height, 2 * SUB)
        for k in range(strip):
            hot_ref[pl.ds(pl.multiple_of(base + k * total, 2 * SUB), height), :] = mark(spread(entry, k), entries)
    logs = dot(hot_ref[:, : 3 * entries], table)
    for k in range(strip):
        cut = logs[k * total : (k + 1) * total]
        raw[3][k * leap : k * leap + total, :] = cut[:, :LANES]
        raw[4][k * leap : k * leap + total, :] = cut[:, LANES:]
    zero = jnp.zeros((SUB, LANES), F32)
    for k in range(count):
        for ref in (ra_ref, rb_ref):
            ref[pl.ds(k * pitch, SUB), :] = zero
            ref[pl.ds(k * pitch + SUB + total, SUB), :] = zero

    for side in (1, 0):
        for d in range(strips):
            base = pl.multiple_of(dest(row, d) * height, SUB) + SUB
            va = blocks[side][d][: count * height, :].astype(F32)
            low, high = unpack(blocks[side][d][count * height : rows, :].astype(F32))
            h2 = height // 2
            for k in range(count):
                to = pl.multiple_of(base + k * pitch, SUB)
                ra_ref[pl.ds(to, height), :] = va[k * height : (k + 1) * height]
                rb_ref[pl.ds(to, h2), :] = low[k * h2 : (k + 1) * h2]
                rb_ref[pl.ds(pl.multiple_of(to + h2, SUB), h2), :] = high[k * h2 : (k + 1) * h2]
        taps = conv_ws[side][...]
        bias = conv_bs[side][...]
        for src, dst, cut in (
            (ra_ref, raw[0], lambda v: v[..., :LANES]),
            (rb_ref, raw[1], lambda v: twice(v[..., LANES:])),
        ):
            cut_taps, add = cut(taps), cut(bias)
            taps_wide = [[jnp.broadcast_to(cut_taps[a, b][None, :], (SUB, LANES)) for b in range(3)] for a in range(3)]
            start = jnp.broadcast_to(add, (SUB, LANES))

            def conv(i, unused, src=src, dst=dst, taps_wide=taps_wide, start=start):
                sums = [start] * strip
                for k in range(count):
                    for a in range(3):
                        v = src[pl.ds(k * pitch + i * SUB + SUB - 1 + a, SUB), :]
                        for b in range(3):
                            if 0 <= k - b < strip:
                                sums[k - b] = sums[k - b] + taps_wide[a][b] * v
                for k in range(strip):
                    v = sums[k] / (1.0 + jnp.exp(-sums[k]))
                    dst[pl.ds(k * leap + i * SUB, SUB), :] = v.astype(BF16).astype(F32)
                return unused

            lax.fori_loop(0, total // SUB, conv, 0)
        proj = thrice(projs[side][...])
        for k in range(strip):
            at = pl.ds(k * leap, total)
            part = dot_t(raw[0][at, :].astype(BF16), proj[:, :LANES]) + dot_t(
                raw[1][at, : LANES // 2].astype(BF16), proj[:, LANES:]
            )
            raw[2][at, : 6 * states] = part if side else part + raw[2][at, : 6 * states]

    skip = skip_ref[...]
    skip_a, skip_b = skip[:, :LANES], twice(skip[:, LANES:])

    def here(h, base=0):
        at = base + h * strip
        return pl.ds(at if strip % SUB else pl.multiple_of(at, SUB), strip)

    def order(h, unused):
        for old, new in zip(raw, (xa_ref, xb_ref, cf_ref, la_ref, lb_ref)):
            new[here(h), :] = old[pl.ds(h, strip, stride=leap), :]
        return unused

    steps(total, order, 0)
    cells = total * strip
    every = [(s, drives.at[s * cells : (s + 1) * cells, :], cells) for s in range(states)]
    every += [(states + s, weights.at[s * cells : (s + 1) * cells, :], cells) for s in range(states)]
    cut = states * 5 // 4 // 2 * 2
    spread_all(cf_ref, 2 * states, every[:cut], every[cut:])

    def body(h, carry):
        at = here(h)
        xa, xb = xa_ref[at, :], xb_ref[at, :]
        carry, ya, yb = advance(
            carry,
            xa,
            xb,
            la_ref[at, :],
            lb_ref[at, :],
            lambda s: drives[here(h, s * cells), :],
            lambda s: weights[here(h, s * cells), :],
            rates,
        )
        ya_ref[at, :] = ya + skip_a * xa
        yb_ref[at, :] = yb + skip_b * xb
        return carry

    zeros = tuple(jnp.zeros((strip, LANES), F32) for _ in range(states + states // 2))
    steps(total, body, zeros)

    cells = height * strip
    for d in range(strips):
        start = pl.multiple_of(dest(row, d) * cells, SUB)
        from_ = pl.ds(start, cells)
        outs[d][:cells, :] = ya_ref[from_, :].astype(BF16)
        yb = yb_ref[from_, :]
        low, high = yb[: cells // 2], yb[cells // 2 :]
        outs[d][cells:, :] = jnp.where(low_half(low.shape), low, high).astype(BF16)


def gate_kernel(dims, dest, *refs):
    strips, height, width, strip = dims
    blocks, gate_ref, out_ref, ya_ref, yb_ref = refs[:strips], *refs[strips:]
    row = lax.axis_index("rows")
    cells = height * strip
    for d in range(strips):
        va = blocks[d][:cells, :].astype(F32)
        low, high = unpack(blocks[d][cells:, :].astype(F32))
        left = dest(row, d) * strip
        for h in range(height):
            to = left + h * width
            to = pl.ds(to if strip % SUB else pl.multiple_of(to, SUB), strip)
            ya_ref[to, :] = va[h * strip : (h + 1) * strip]
            b, i = (low, h) if h < height // 2 else (high, h - height // 2)
            yb_ref[to, :] = b[i * strip : (i + 1) * strip]
    gate = gate_ref[...].astype(F32)
    gate = gate / (1.0 + jnp.exp(-gate))
    out_ref[:, :, :LANES] = (ya_ref[...].reshape(height, width, LANES) * gate[:, :, :LANES]).astype(BF16)
    yb = yb_ref[...].reshape(height, width, LANES)[:, :, : LANES // 2]
    out_ref[:, :, LANES:] = (yb * gate[:, :, LANES:]).astype(BF16)


def smem():
    return pl.BlockSpec(memory_space=pltpu.SMEM)


def hbm():
    return pl.BlockSpec(memory_space=pltpu.HBM)


def vmem():
    return pl.BlockSpec(memory_space=pltpu.VMEM)


def call(kernel, args, outs, scratch, limit, left=False):
    held = []
    if left:
        args = [pltpu.with_memory_space_constraint(a, pltpu.HBM) for a in args]
        held = [(pltpu.SMEM if a.ndim == 1 else pltpu.VMEM)(a.shape, a.dtype) for a in args]
        held += [pltpu.SemaphoreType.DMA((len(args),))]
    return pl.pallas_call(
        kernel,
        out_shape=outs,
        in_specs=[hbm() if left else smem() if a.ndim == 1 else vmem() for a in args],
        out_specs=jax.tree.map(lambda _: vmem(), outs),
        scratch_shapes=[pltpu.VMEM(getattr(s, "shape", s), getattr(s, "dtype", F32)) for s in scratch] + held,
        compiler_params=pltpu.CompilerParams(vmem_limit_bytes=limit),
    )(*args)


def make_shards(strips, tiles):
    few = strips <= 8 and strips & (strips - 1) == 0
    swap = [(0, 1), (1, 0)]

    def dest(row, d):
        return row ^ d if few else d

    def exchange(blocks, axis="rows"):
        if few:
            moved = [blocks[0]]
            for d in range(1, strips):
                moved.append(lax.ppermute(blocks[d], axis, [(i, i ^ d) for i in range(strips)]))
            return moved
        moved = lax.all_to_all(jnp.stack(blocks), axis, 0, 0)
        return [moved[d] for d in range(strips)]

    def across(v):
        return lax.ppermute(v, "chan", swap)

    def shards(features, gate, decay_idx, log_table, rate, proj_row, proj_col, conv_w, conv_b, d_skip):
        height, width, channels = features.shape
        states = rate.shape[0]
        strip = width // strips
        cells, total, count = height * width, strips * height, strip + 2
        skip, bias = d_skip.reshape(1, channels), conv_b.reshape(1, channels)
        proj_row, proj_col = proj_row.T, proj_col.T

        block = jax.ShapeDtypeStruct((count * height * 3 // 2 + height, LANES), BF16)
        kinds = states * 3 // 2
        rate_rows = (kinds * SUB, LANES)
        high = pitch_of(width) * height
        other = [across(features)]
        proj_row2 = across(proj_row)
        if tiles == 2:
            wide = jax.ShapeDtypeStruct((cells, LANES), F32)
            rates = jax.ShapeDtypeStruct(rate_rows, F32)
            entries = log_table.shape[0]
            xa, xb, la, lb, half, rates, skips, entry, marks = call(
                lambda *r: own_kernel((height, width), *r),
                [rate, features, decay_idx, log_table, proj_row, skip],
                [wide] * 5
                + [
                    rates,
                    jax.ShapeDtypeStruct((2 * SUB, LANES), F32),
                    jax.ShapeDtypeStruct((height, LANES), F32),
                    jax.ShapeDtypeStruct((3 * entries, 2 * LANES), BF16),
                ],
                [(high, LANES)] * 3 + [jax.ShapeDtypeStruct((cells, LANES), BF16)],
                8 << 20,
                left=True,
            )
            note, ta, tb, sa, sb, cf = call(
                lambda *r: tile_kernel((height, width), *r),
                [other[0], proj_row2, xa, xb, la, lb, half, rates, skips, entry],
                [jax.ShapeDtypeStruct(((kinds + 6) * height, LANES), BF16)] + [wide] * 5,
                [(high, LANES)] + [(states * cells, LANES)] * 2,
                16 << 20,
            )
            came = lax.ppermute(note, "cols", swap)
            brings = call(
                lambda *r: weigh_kernel(*r),
                [cf, sa, sb, rates],
                jax.ShapeDtypeStruct((kinds * cells, LANES), F32),
                [(states * cells, LANES)],
                16 << 20,
            )
            sent = call(
                lambda *r: join_kernel((strips, height, width, strip), dest, *r),
                [note, came, ta, tb, brings, entry, marks, rates],
                [block] * strips,
                [((width + 2) * height, LANES)] * 2,
                8 << 20,
            )
        else:
            rounds = [[(i, (i + d) % tiles) for i in range(tiles)] for d in range(1, tiles)]
            own = [features] + [lax.ppermute(features, "cols", pairs) for pairs in rounds]
            idx = [decay_idx] + [lax.ppermute(decay_idx, "cols", pairs) for pairs in rounds]
            other += [across(f) for f in own[1:]]
            sent = call(
                lambda *r: row_kernel((tiles, strips, height, width, strip), dest, *r),
                [rate, *own, *other, *idx, log_table, proj_row, proj_row2, skip],
                [block] * strips,
                [(tiles * high, LANES)] * 3
                + [(tiles * cells, LANES)] * 5
                + [(states * tiles * cells, LANES), (states * cells, LANES)]
                + [((width + 2) * height, LANES)] * 2
                + [rate_rows, (height, LANES), jax.ShapeDtypeStruct((cells, LANES), BF16)],
                40 << 20,
            )
        proj_col2, conv_w2, bias2 = across(proj_col), across(conv_w), across(bias)
        got = exchange(sent)
        got2 = [across(b) for b in got]
        back = jax.ShapeDtypeStruct((height * strip * 3 // 2, LANES), BF16)
        pitch = total + 2 * SUB
        sent = call(
            lambda *r: column_kernel((strips, height, strip), dest, *r),
            [rate, *got, *got2, log_table, proj_col, proj_col2, conv_w, conv_w2, bias, bias2, skip],
            [back] * strips,
            [(count * pitch, LANES)] * 2
            + [(strip * pitch_of(total), LANES)] * 5
            + [(total * strip, LANES)] * 7
            + [(states * total * strip, LANES)] * 2
            + [(states * 3 // 2 * SUB, LANES), jax.ShapeDtypeStruct((total * strip, LANES), BF16)],
            20 << 20,
        )
        got = exchange(sent)
        return call(
            lambda *r: gate_kernel((strips, height, width, strip), dest, *r),
            [*got, gate],
            jax.ShapeDtypeStruct(features.shape, BF16),
            [(cells, LANES)] * 2,
            8 << 20,
        )

    return shards


def solution(mesh):
    placed = (
        P(("slides", "rows"), "cols", "chan"),
        P(("slides", "rows"), "cols", "chan"),
        P(("slides", "rows"), "cols"),
        P(None, "chan"),
        P(),
        P("chan", None),
        P("chan", None),
        P(None, None, "chan"),
        P("chan"),
        P("chan"),
    )
    shards = make_shards(mesh.shape["rows"], mesh.shape["cols"])

    return jax.shard_map(
        shards, mesh=mesh, in_specs=placed, out_specs=P(("slides", "rows"), "cols", "chan"), check_vma=False
    )
```

```python
import jax
import jax.numpy as jnp
from jax import lax
from jax.experimental import pallas as pl
from jax.experimental.pallas import tpu as pltpu
from jax.sharding import PartitionSpec as P


LANES = 128
SUB = 8
UNROLL = 8
LOG2E = 1.4426950408889634
F32 = jnp.float32
BF16 = jnp.bfloat16


def low_half(shape):
    return lax.broadcasted_iota(jnp.int32, shape, len(shape) - 1) < LANES // 2


def twice(v):
    return jnp.concatenate([v, v], axis=-1)


def split3(t):
    hi = t.astype(BF16)
    rest = t - hi.astype(F32)
    mid = rest.astype(BF16)
    low = (rest - mid.astype(F32)).astype(BF16)
    return jnp.concatenate([hi, mid, low], axis=0)


def tables(table_ref):
    t = table_ref[...] * LOG2E
    return split3(jnp.concatenate([t[:, :LANES], twice(t[:, LANES:])], axis=-1))


def mark(entry, entries):
    lane = lax.broadcasted_iota(jnp.int32, entry.shape, 1)
    spot = jnp.where(lane < 3 * entries, lane % entries, -1).astype(F32)
    return (entry == spot).astype(F32).astype(BF16)


def dot(a, b):
    return jnp.dot(a, b, preferred_element_type=F32)


def dot_t(a, b):
    return lax.dot_general(a, b, (((1,), (1,)), ((), ())), preferred_element_type=F32)


def fill_rates(rate_ref, rates):
    half = low_half((SUB, LANES))
    states = rate_ref.shape[0]
    for s in range(states):
        rates[s * SUB : (s + 1) * SUB, :] = jnp.full((SUB, LANES), rate_ref[s], F32)
    for j in range(states // 2):
        at = (states + j) * SUB
        rates[at : at + SUB, :] = jnp.where(half, rate_ref[2 * j], rate_ref[2 * j + 1])


def steps(count, step, carry):
    first = count % UNROLL
    for i in range(first):
        carry = step(i, carry)

    def body(i, carry):
        for k in range(UNROLL):
            carry = step(first + i * UNROLL + k, carry)
        return carry

    return lax.fori_loop(0, count // UNROLL, body, carry)


def pitch_of(rows):
    return rows + SUB // 2 if rows % SUB == 0 else rows


def advance(carry, xa, xb, decay, drive, out):
    states = len(carry) * 2 // 3
    half = low_half(xa.shape)
    drive = [drive(s) for s in range(states)]
    out = None if out is None else [out(s) for s in range(states)]
    new, ya, yb = [], [], []
    for s in range(states):
        st = decay(s) * carry[s] + drive[s] * xa
        new.append(st)
        if out:
            ya.append(out[s] * st)
    for j in range(states // 2):
        b = jnp.where(half, drive[2 * j], drive[2 * j + 1])
        st = decay(states + j) * carry[states + j] + b * xb
        new.append(st)
        if out:
            yb.append(jnp.where(half, out[2 * j], out[2 * j + 1]) * st)

    def tree(v):
        while len(v) > 1:
            v = [v[i] + v[i + 1] for i in range(0, len(v) - 1, 2)] + v[len(v) & ~1 :]
        return v[0] if v else None

    yb = tree(yb)
    return tuple(new), tree(ya), None if yb is None else yb + pltpu.roll(yb, LANES // 2, 1)


def decays(la, lb, rates):
    kinds = rates.shape[0] // SUB
    rows = la.shape[0]
    return lambda k: jnp.exp2((la if k < kinds * 2 // 3 else lb) * rates[k * SUB : k * SUB + rows, :])


def spread(coeff, column):
    return jnp.broadcast_to(coeff[:, column : column + 1], (coeff.shape[0], LANES))


def thirds(v, count):
    lane = lax.broadcasted_iota(jnp.int32, v.shape, 1)
    hi = v.astype(BF16).astype(F32)
    mid = (v - hi).astype(BF16).astype(F32)
    return jnp.where(lane < count, hi, jnp.where(lane < 2 * count, mid, v - hi - mid))


def spread_all(cf_ref, count, matrix, permute):
    for (column, to, rows), (column2, to2, rows2) in zip(matrix[::2], matrix[1::2]):
        parts = thirds(cf_ref[:rows, : 3 * count], count).astype(BF16)
        shape = (3 * count, 2 * LANES)
        source = lax.broadcasted_iota(jnp.int32, shape, 0) % count
        wanted = jnp.where(lax.broadcasted_iota(jnp.int32, shape, 1) < LANES, column, column2)
        wide = dot(parts, (source == wanted).astype(BF16))
        to[...] = wide[:, :LANES]
        to2[...] = wide[:, LANES:]
    for column, to, rows in permute:
        to[...] = spread(cf_ref[:rows, :], column)


def fill(v):
    return jnp.concatenate([v] * (LANES // v.shape[0]), axis=0)


def row_kernel(dims, dest, *refs):
    tiles, strips, height, width, strip = dims
    rate_ref = refs[0]
    own, other = refs[1 : 1 + tiles], refs[1 + tiles : 1 + 2 * tiles]
    idxs = refs[1 + 2 * tiles : 1 + 3 * tiles]
    table_ref, proj_ref, proj2_ref, skip_ref = refs[1 + 3 * tiles : 5 + 3 * tiles]
    outs = refs[5 + 3 * tiles : 5 + 3 * tiles + strips]
    scratch = refs[5 + 3 * tiles + strips :]
    raw, xa_ref, xb_ref, la_ref, lb_ref, cf_ref, drives, weights, ya_ref, yb_ref, rates = scratch[:3], *scratch[3:13]
    entry_ref, hot_ref = scratch[13:]
    states = rate_ref.shape[0]
    cells = height * width
    pitch = pitch_of(width)
    col = lax.axis_index("cols")
    row = lax.axis_index("rows")

    table = tables(table_ref)
    entries = table_ref.shape[0]
    entry_ref[...] = jnp.zeros(entry_ref.shape, F32)
    proj, proj2 = fill(proj_ref[...]), fill(proj2_ref[...])
    for d in range(tiles):
        x = own[d][...].reshape(cells, -1)
        part = pl.ds(d * cells, cells)
        coeff = dot_t(x, proj) + dot_t(other[d][...].reshape(cells, -1), proj2)
        xf = x.astype(F32)
        xa, xb = xf[:, :LANES], twice(xf[:, LANES:])
        if 0 < d < tiles - 1:
            there = (col >= d).astype(F32)
            xa, xb = xa * there, xb * there
        for h in range(height):
            to, cut = pl.ds((d * height + h) * pitch, width), slice(h * width, (h + 1) * width)
            raw[0][to, :] = xa[cut]
            raw[1][to, :] = xb[cut]
            raw[2][to, :] = coeff[cut]
        entry = idxs[d][...].astype(F32)
        if d == 0:
            entry_ref[:, :width] = entry
        for w in range(width):
            hot_ref[w * height : (w + 1) * height, :] = mark(spread(entry, w), entries)
        logs = dot(hot_ref[:, : 3 * entries], table)
        la_ref[part, :] = logs[:, :LANES]
        lb_ref[part, :] = logs[:, LANES:]

    fill_rates(rate_ref, rates)
    for d in range(tiles):

        def order(w, unused, d=d):
            for g in range(height // SUB):
                place = pl.ds((d * height + g * SUB) * pitch + w, SUB, stride=pitch)
                to = pl.ds(pl.multiple_of(d * cells + w * height + g * SUB, SUB), SUB)
                for old, new in zip(raw, (xa_ref, xb_ref, cf_ref)):
                    new[to, :] = old[place, :]
            return unused

        steps(width, order, 0)
    size = tiles * cells
    every = [(s, drives.at[s * size : (s + 1) * size, :], size) for s in range(states)]
    every += [(states + s, weights.at[s * cells : (s + 1) * cells, :], cells) for s in range(states)]
    cut = states * 7 // 8 // 2 * 2
    spread_all(cf_ref, 2 * states, every[:cut], every[cut:])

    skip = skip_ref[...]
    skip_a, skip_b = skip[:, :LANES], twice(skip[:, LANES:])
    last_left = (col >= tiles - 1).astype(F32)

    for g in range(height // SUB):

        def step(carry, d, w, wanted, g=g):
            here = w * height + g * SUB
            at = pl.ds(pl.multiple_of(d * cells + here, SUB), SUB)
            xa, xb = xa_ref[at, :], xb_ref[at, :]

            def drive(s):
                return drives[pl.ds(pl.multiple_of((s * tiles + d) * cells + here, SUB), SUB), :]

            def out(s):
                if d:
                    return spread(cf_ref[at, :], states + s)
                return weights[pl.ds(pl.multiple_of(s * cells + here, SUB), SUB), :]

            carry, ya, yb = advance(
                carry, xa, xb, decays(la_ref[at, :], lb_ref[at, :], rates), drive, out if wanted else None
            )
            if wanted:
                ya, yb = ya + skip_a * xa, yb + skip_b * xb
            return carry, ya, yb

        def put(c, ya, yb, g=g):
            at = pl.ds(pl.multiple_of(c * height + g * SUB, SUB), SUB)
            ya_ref[at, :] = ya
            yb_ref[at, :] = yb

        carry = tuple(jnp.zeros((SUB, LANES), F32) for _ in range(states + states // 2))
        for d in range(tiles - 1, 0, -1):
            carry = steps(width - (d == 1), lambda w, s, d=d: step(s, d, w, False)[0], carry)
            if d == tiles - 1:
                carry = tuple(v * last_left for v in carry)
        carry, ya, yb = step(carry, 1, width - 1, True)
        if tiles == 2:
            carry = tuple(v * last_left for v in carry)
            ya, yb = ya * last_left, yb * last_left
        put(0, ya, yb)

        def body(w, s):
            s, ya, yb = step(s, 0, w, True)
            put(w + 1, ya, yb)
            return s

        carry = steps(width, body, carry)
        _, ya, yb = step(carry, tiles - 1, 0, True)
        inside = 1.0 - last_left
        put(width + 1, ya * inside, yb * inside)

    pack_blocks(outs, dest, row, strip, height, ya_ref, yb_ref, entry_ref)


def pack_blocks(outs, dest, row, strip, height, ya_ref, yb_ref, entry_ref):
    count = strip + 2
    rows = count * height * 3 // 2
    for d in range(len(outs)):
        start = pl.multiple_of(dest(row, d) * strip * height, SUB)
        from_ = pl.ds(start, count * height)
        outs[d][: count * height, :] = ya_ref[from_, :].astype(BF16)
        yb = yb_ref[from_, :].reshape(count, 2, height // 2, LANES)
        low, high = yb[:, 0], yb[:, 1]
        packed = jnp.where(low_half(low.shape), low, high).reshape(count * height // 2, LANES)
        outs[d][count * height : rows, :] = packed.astype(BF16)
        entry = pltpu.roll(entry_ref[...], LANES - dest(row, d) * strip, 1)
        outs[d][rows:, :] = entry.astype(BF16)


def split2(v):
    hi = v.astype(BF16).astype(F32)
    return hi, v - hi


def own_kernel(dims, *refs):
    height, width = dims
    inputs, (xa_ref, xb_ref, la_ref, lb_ref, cf_ref, rates, skips, entry_ref, marks) = refs[:6], refs[6:15]
    raw, hot_ref, held, arrived = refs[15:18], refs[18], refs[19:25], refs[25]
    copies = [pltpu.make_async_copy(a, b, arrived.at[i]) for i, (a, b) in enumerate(zip(inputs, held))]
    for copy in copies:
        copy.start()
    for copy in copies:
        copy.wait()
    rate_ref, own_ref, idx_ref, table_ref, proj_ref, skip_ref = held
    cells = height * width
    pitch = pitch_of(width)

    table = tables(table_ref)
    marks[...] = table
    entries = table_ref.shape[0]
    x = own_ref[...].reshape(cells, -1)
    coeff = dot_t(x, fill(proj_ref[...]))
    xf = x.astype(F32)
    xa, xb = xf[:, :LANES], twice(xf[:, LANES:])
    for h in range(height):
        to, cut = pl.ds(h * pitch, width), slice(h * width, (h + 1) * width)
        raw[0][to, :] = xa[cut]
        raw[1][to, :] = xb[cut]
        raw[2][to, :] = coeff[cut]
    entry = idx_ref[...].astype(F32)
    entry_ref[...] = jnp.zeros(entry_ref.shape, F32)
    entry_ref[:, :width] = entry
    for w in range(width):
        hot_ref[w * height : (w + 1) * height, :] = mark(spread(entry, w), entries)
    logs = dot(hot_ref[:, : 3 * entries], table)
    la_ref[...] = logs[:, :LANES]
    lb_ref[...] = logs[:, LANES:]
    fill_rates(rate_ref, rates)
    skip = skip_ref[...]
    skips[:SUB, :] = jnp.broadcast_to(skip[:, :LANES], (SUB, LANES))
    skips[SUB:, :] = jnp.broadcast_to(twice(skip[:, LANES:]), (SUB, LANES))
    in_order(dims, raw, (xa_ref, xb_ref, cf_ref))


def in_order(dims, olds, news, add=None):
    height, width = dims
    pitch = pitch_of(width)

    def order(w, unused):
        for g in range(height // SUB):
            place = pl.ds(g * SUB * pitch + w, SUB, stride=pitch)
            to = pl.ds(pl.multiple_of(w * height + g * SUB, SUB), SUB)
            for old, new in zip(olds, news):
                new[to, :] = old[place, :] if add is None else old[place, :] + add[to, :]
        return unused

    steps(width, order, 0)


def add_up(v):
    while len(v) > 1:
        v = [v[i] + v[i + 1] for i in range(0, len(v) - 1, 2)] + v[len(v) & ~1 :]
    return v[0]


def at_step(ref, i, cells, here):
    return ref[pl.ds(pl.multiple_of(i * cells + here, SUB), SUB), :]


def tile_kernel(dims, *refs):
    height, width = dims
    other_ref, proj2_ref, xa_ref, xb_ref, la_ref, lb_ref, half_ref, rates, skips, entry_ref = refs[:10]
    note_ref, ya_ref, yb_ref, sa_ref, sb_ref, cf_ref = refs[10:16]
    raw, drives, weights = refs[16:]
    kinds = rates.shape[0] // SUB
    states = kinds * 2 // 3
    cells = height * width
    pitch = pitch_of(width)

    coeff = dot_t(other_ref[...].reshape(cells, -1), fill(proj2_ref[...]))
    for h in range(height):
        raw[h * pitch : h * pitch + width, :] = coeff[h * width : (h + 1) * width]
    in_order(dims, (raw,), (cf_ref,), half_ref)
    every = [(s, drives.at[s * cells : (s + 1) * cells, :], cells) for s in range(states)]
    every += [(states + s, weights.at[s * cells : (s + 1) * cells, :], cells) for s in range(states)]
    cut = states * 5 // 4 // 2 * 2
    spread_all(cf_ref, 2 * states, every[:cut], every[cut:])

    skip_a, skip_b = skips[:SUB, :], skips[SUB:, :]
    for g in range(height // SUB):

        def step(w, carry, g=g):
            carry, sum_a, sum_b = carry
            here = w * height + g * SUB
            at = pl.ds(pl.multiple_of(here, SUB), SUB)
            xa, xb, la, lb = xa_ref[at, :], xb_ref[at, :], la_ref[at, :], lb_ref[at, :]
            carry, ya, yb = advance(
                carry,
                xa,
                xb,
                decays(la, lb, rates),
                lambda s: at_step(drives, s, cells, here),
                lambda s: at_step(weights, s, cells, here),
            )
            sum_a, sum_b = sum_a + la, sum_b + lb
            ya_ref[at, :] = ya + skip_a * xa
            yb_ref[at, :] = yb + skip_b * xb
            sa_ref[at, :] = sum_a
            sb_ref[at, :] = sum_b
            return carry, sum_a, sum_b

        zero = jnp.zeros((SUB, LANES), F32)
        carry, _, _ = steps(width, step, ((zero,) * kinds, zero, zero))
        for i in range(0, kinds, 2):
            at = (g * kinds + i) * SUB
            note_ref[at : at + 2 * SUB, :] = jnp.concatenate(carry[i : i + 2], axis=0).astype(BF16)

    lane = lax.broadcasted_iota(jnp.int32, (height, LANES), 1)
    first = jnp.where(lane < 6 * states, thirds(cf_ref[:height, :], 2 * states), 0.0)
    a, a2 = split2(ya_ref[:height, :])
    b, b2 = split2(yb_ref[:height, :])
    extra = [
        jnp.where(lane == 6 * states, spread(entry_ref[...], 0), first),
        a,
        a2,
        jnp.where(low_half(b.shape), b, b2),
        ya_ref[cells - height :, :],
        yb_ref[cells - height :, :],
    ]
    for i, v in enumerate(extra):
        at = kinds * height + i * height
        note_ref[at : at + height, :] = v.astype(BF16)


def weigh_kernel(*refs):
    cf_ref, sa_ref, sb_ref, rates, out_ref, weights = refs
    kinds = rates.shape[0] // SUB
    states = kinds * 2 // 3
    cells = cf_ref.shape[0]
    half = low_half((SUB, LANES))
    every = [(states + s, weights.at[s * cells : (s + 1) * cells, :], cells) for s in range(states)]
    cut = states * 5 // 8 // 2 * 2
    spread_all(cf_ref, 2 * states, every[:cut], every[cut:])

    def step(i, unused):
        here = i * SUB
        at = pl.ds(pl.multiple_of(here, SUB), SUB)
        sum_a, sum_b = sa_ref[at, :], sb_ref[at, :]
        wide = [at_step(weights, s, cells, here) for s in range(states)]
        for k in range(kinds):
            j = k - states
            log, weight = (sum_a, wide[k]) if j < 0 else (sum_b, jnp.where(half, wide[2 * j], wide[2 * j + 1]))
            to = pl.ds(pl.multiple_of(k * cells + here, SUB), SUB)
            out_ref[to, :] = weight * jnp.exp2(log * rates[k * SUB : (k + 1) * SUB, :])
        return unused

    steps(cells // SUB, step, 0)


def join_kernel(dims, dest, *refs):
    strips, height, width, strip = dims
    own_ref, came_ref, ta_ref, tb_ref, brings, entry_ref, marks, rates = refs[:8]
    outs = refs[8 : 8 + strips]
    ya_ref, yb_ref = refs[8 + strips :]
    kinds = rates.shape[0] // SUB
    states = kinds * 2 // 3
    cells = height * width
    row = lax.axis_index("rows")
    right = (lax.axis_index("cols") == 1).astype(F32)
    half = low_half((SUB, LANES))

    def extra(i):
        at = (kinds + i) * height
        return came_ref[at : at + height, :].astype(F32)

    first = extra(0)
    log = dot(mark(spread(first, 6 * states), marks.shape[0] // 3)[:, : marks.shape[0]], marks[...])
    group = 2 * states
    coeff = first + pltpu.roll(first, LANES - group, 1) + pltpu.roll(first, LANES - 2 * group, 1)
    near_b = extra(3)
    near_b = near_b + pltpu.roll(near_b, LANES // 2, 1)
    near_a = extra(1) + extra(2)
    ya_ref[:height, :] = extra(4) * right
    yb_ref[:height, :] = extra(5) * right

    for g in range(height // SUB):

        def inflow(ref, scale, g=g):
            new = []
            for i in range(0, kinds, 2):
                at = (g * kinds + i) * SUB
                v = ref[at : at + 2 * SUB, :].astype(F32) * scale
                new += [v[:SUB], v[SUB:]]
            return tuple(new)

        def step(w, state, g=g):
            here = w * height + g * SUB
            at = pl.ds(pl.multiple_of(here, SUB), SUB)
            to = pl.ds(pl.multiple_of(here + height, SUB), SUB)
            terms = [at_step(brings, k, cells, here) * state[k] for k in range(kinds)]
            b = add_up(terms[states:])
            ya_ref[to, :] = ta_ref[at, :] + add_up(terms[:states])
            yb_ref[to, :] = tb_ref[at, :] + b + pltpu.roll(b, LANES // 2, 1)
            return state

        steps(width, step, inflow(came_ref, right))
        cut = slice(g * SUB, (g + 1) * SUB)
        state = inflow(own_ref, 1.0)
        wide = [spread(coeff[cut], states + s) for s in range(states)]
        wide += [jnp.where(half, wide[2 * j], wide[2 * j + 1]) for j in range(states // 2)]
        terms = []
        for k in range(kinds):
            part = log[cut, :LANES] if k < states else log[cut, LANES:]
            terms.append(wide[k] * (jnp.exp2(part * rates[k * SUB : (k + 1) * SUB, :]) * state[k]))
        b = add_up(terms[states:])
        at = slice((width + 1) * height + g * SUB, (width + 1) * height + (g + 1) * SUB)
        ya_ref[at, :] = (near_a[cut] + add_up(terms[:states])) * (1.0 - right)
        yb_ref[at, :] = (near_b[cut] + b + pltpu.roll(b, LANES // 2, 1)) * (1.0 - right)

    pack_blocks(outs, dest, row, strip, height, ya_ref, yb_ref, entry_ref)


def unpack(v):
    half = low_half(v.shape)
    turned = pltpu.roll(v, LANES // 2, 1)
    return jnp.where(half, v, turned), jnp.where(half, turned, v)


def conv_kernel(dims, dest, *refs):
    strips, height, strip = dims
    blocks, (conv_ref, bias_ref, proj_ref) = refs[:strips], refs[strips : strips + 3]
    mids, cf_ref, rows_refs = refs[strips + 3 : strips + 5], refs[strips + 5], refs[strips + 6 :]
    row = lax.axis_index("rows")
    total = strips * height
    pitch = total + 2 * SUB
    leap = pitch_of(total)
    count = strip + 2
    half = height // 2
    rows = count * height * 3 // 2

    zero = jnp.zeros((SUB, LANES), F32)
    for k in range(count):
        for ref in rows_refs:
            ref[pl.ds(k * pitch, SUB), :] = zero
            ref[pl.ds(k * pitch + SUB + total, SUB), :] = zero
    for d in range(strips):
        base = pl.multiple_of(dest(row, d) * height, SUB) + SUB
        va = blocks[d][: count * height, :].astype(F32)
        low, high = unpack(blocks[d][count * height : rows, :].astype(F32))
        for k in range(count):
            to = pl.multiple_of(base + k * pitch, SUB)
            rows_refs[0][pl.ds(to, height), :] = va[k * height : (k + 1) * height]
            rows_refs[1][pl.ds(to, half), :] = low[k * half : (k + 1) * half]
            rows_refs[1][pl.ds(pl.multiple_of(to + half, SUB), half), :] = high[k * half : (k + 1) * half]
    taps = conv_ref[...]
    bias = bias_ref[...]
    for src, dst, cut in zip(rows_refs, mids, (lambda v: v[..., :LANES], lambda v: twice(v[..., LANES:]))):
        cut_taps, add = cut(taps), cut(bias)
        taps_wide = [[jnp.broadcast_to(cut_taps[a, b][None, :], (SUB, LANES)) for b in range(3)] for a in range(3)]
        start = jnp.broadcast_to(add, (SUB, LANES))

        def conv(i, unused, src=src, dst=dst, taps_wide=taps_wide, start=start):
            sums = [start] * strip
            for k in range(count):
                for a in range(3):
                    v = src[pl.ds(k * pitch + i * SUB + SUB - 1 + a, SUB), :]
                    for b in range(3):
                        if 0 <= k - b < strip:
                            sums[k - b] = sums[k - b] + taps_wide[a][b] * v
            for k in range(strip):
                v = sums[k] / (1.0 + jnp.exp(-sums[k]))
                dst[pl.ds(k * leap + i * SUB, SUB), :] = v.astype(BF16).astype(F32)
            return unused

        lax.fori_loop(0, total // SUB, conv, 0)
    proj = fill(proj_ref[...])
    for k in range(strip):
        at = pl.ds(k * leap, total)
        cf_ref[at, :] = dot_t(mids[0][at, :].astype(BF16), proj[:, :LANES]) + dot_t(
            mids[1][at, : LANES // 2].astype(BF16), proj[:, LANES:]
        )


def strip_at(h, strip, base=0):
    at = base + h * strip
    return pl.ds(at if strip % SUB else pl.multiple_of(at, SUB), strip)


def decay_kernel(dims, dest, *refs):
    strips, height, strip = dims
    blocks, mids, marks, rates = refs[:strips], refs[strips : strips + 2], refs[strips + 2], refs[strips + 3]
    xa_ref, xb_ref, out_ref = refs[strips + 4 : strips + 7]
    raw, hot_ref = refs[strips + 7 : strips + 9], refs[strips + 9]
    row = lax.axis_index("rows")
    total = strips * height
    leap = pitch_of(total)
    cells = total * strip
    kinds = rates.shape[0] // SUB
    parts = marks.shape[0]
    rows = (strip + 2) * height * 3 // 2
    for d in range(strips):
        entry = blocks[d][rows:, :].astype(F32)
        base = pl.multiple_of(dest(row, d) * height, 2 * SUB)
        for k in range(strip):
            to = pl.ds(pl.multiple_of(base + k * total, 2 * SUB), height)
            hot_ref[to, :] = mark(spread(entry, k), parts // 3)
    logs = dot(hot_ref[:, :parts], marks[...])
    for k in range(strip):
        cut, at = logs[k * total : (k + 1) * total], pl.ds(k * leap, total)
        raw[0][at, :] = cut[:, :LANES]
        raw[1][at, :] = cut[:, LANES:]

    def step(h, unused):
        place = pl.ds(h, strip, stride=leap)
        at = strip_at(h, strip)
        xa_ref[at, :] = mids[0][place, :]
        xb_ref[at, :] = mids[1][place, :]
        decay = decays(raw[0][place, :], raw[1][place, :], rates)
        for k in range(kinds):
            out_ref[strip_at(h, strip, k * cells), :] = decay(k)
        return unused

    steps(total, step, 0)


def column_kernel(dims, dest, *refs):
    strips, height, strip = dims
    own_ref, came_ref, xa_ref, xb_ref, decay_ref, skips = refs[:6]
    outs = refs[6 : 6 + strips]
    cf_ref, ya_ref, yb_ref, drives, weights = refs[6 + strips :]
    row = lax.axis_index("rows")
    total = strips * height
    leap = pitch_of(total)
    cells = total * strip
    states = weights.shape[0] // cells

    def order(h, unused):
        place = pl.ds(h, strip, stride=leap)
        cf_ref[strip_at(h, strip), :] = own_ref[place, :] + came_ref[place, :]
        return unused

    steps(total, order, 0)
    every = [(s, drives.at[s * cells : (s + 1) * cells, :], cells) for s in range(states)]
    every += [(states + s, weights.at[s * cells : (s + 1) * cells, :], cells) for s in range(states)]
    cut = states * 5 // 4 // 2 * 2
    spread_all(cf_ref, 2 * states, every[:cut], every[cut:])
    skip_a, skip_b = skips[:strip, :], skips[SUB : SUB + strip, :]

    def step(h, carry):
        at = strip_at(h, strip)
        xa, xb = xa_ref[at, :], xb_ref[at, :]
        carry, ya, yb = advance(
            carry,
            xa,
            xb,
            lambda k: decay_ref[strip_at(h, strip, k * cells), :],
            lambda s: drives[strip_at(h, strip, s * cells), :],
            lambda s: weights[strip_at(h, strip, s * cells), :],
        )
        ya_ref[at, :] = ya + skip_a * xa
        yb_ref[at, :] = yb + skip_b * xb
        return carry

    steps(total, step, tuple(jnp.zeros((strip, LANES), F32) for _ in range(states * 3 // 2)))
    cells = height * strip
    for d in range(strips):
        from_ = pl.ds(pl.multiple_of(dest(row, d) * cells, SUB), cells)
        outs[d][:cells, :] = ya_ref[from_, :].astype(BF16)
        yb = yb_ref[from_, :]
        low, high = yb[: cells // 2], yb[cells // 2 :]
        outs[d][cells:, :] = jnp.where(low_half(low.shape), low, high).astype(BF16)


def gate_kernel(dims, dest, *refs):
    strips, height, width, strip = dims
    blocks, gate_ref, out_ref, ya_ref, yb_ref = refs[:strips], *refs[strips:]
    row = lax.axis_index("rows")
    cells = height * strip
    for d in range(strips):
        va = blocks[d][:cells, :].astype(F32)
        low, high = unpack(blocks[d][cells:, :].astype(F32))
        left = dest(row, d) * strip
        for h in range(height):
            to = left + h * width
            to = pl.ds(to if strip % SUB else pl.multiple_of(to, SUB), strip)
            ya_ref[to, :] = va[h * strip : (h + 1) * strip]
            b, i = (low, h) if h < height // 2 else (high, h - height // 2)
            yb_ref[to, :] = b[i * strip : (i + 1) * strip]
    gate = gate_ref[...].astype(F32)
    gate = gate / (1.0 + jnp.exp(-gate))
    out_ref[:, :, :LANES] = (ya_ref[...].reshape(height, width, LANES) * gate[:, :, :LANES]).astype(BF16)
    yb = yb_ref[...].reshape(height, width, LANES)[:, :, : LANES // 2]
    out_ref[:, :, LANES:] = (yb * gate[:, :, LANES:]).astype(BF16)


def smem():
    return pl.BlockSpec(memory_space=pltpu.SMEM)


def hbm():
    return pl.BlockSpec(memory_space=pltpu.HBM)


def vmem():
    return pl.BlockSpec(memory_space=pltpu.VMEM)


def call(kernel, args, outs, scratch, limit, left=False):
    held = []
    if left:
        args = [pltpu.with_memory_space_constraint(a, pltpu.HBM) for a in args]
        held = [(pltpu.SMEM if a.ndim == 1 else pltpu.VMEM)(a.shape, a.dtype) for a in args]
        held += [pltpu.SemaphoreType.DMA((len(args),))]
    return pl.pallas_call(
        kernel,
        out_shape=outs,
        in_specs=[hbm() if left else smem() if a.ndim == 1 else vmem() for a in args],
        out_specs=jax.tree.map(lambda _: vmem(), outs),
        scratch_shapes=[pltpu.VMEM(getattr(s, "shape", s), getattr(s, "dtype", F32)) for s in scratch] + held,
        compiler_params=pltpu.CompilerParams(vmem_limit_bytes=limit),
    )(*args)


def make_shards(strips, tiles):
    few = strips <= 8 and strips & (strips - 1) == 0
    swap = [(0, 1), (1, 0)]

    def dest(row, d):
        return row ^ d if few else d

    def exchange(blocks, axis="rows"):
        if few:
            moved = [blocks[0]]
            for d in range(1, strips):
                moved.append(lax.ppermute(blocks[d], axis, [(i, i ^ d) for i in range(strips)]))
            return moved
        moved = lax.all_to_all(jnp.stack(blocks), axis, 0, 0)
        return [moved[d] for d in range(strips)]

    def across(v):
        return lax.ppermute(v, "chan", swap)

    def shards(features, gate, decay_idx, log_table, rate, proj_row, proj_col, conv_w, conv_b, d_skip):
        height, width, channels = features.shape
        states = rate.shape[0]
        strip = width // strips
        cells, total, count = height * width, strips * height, strip + 2
        skip, bias = d_skip.reshape(1, channels), conv_b.reshape(1, channels)
        proj_row, proj_col = proj_row.T, proj_col.T

        block = jax.ShapeDtypeStruct((count * height * 3 // 2 + height, LANES), BF16)
        kinds = states * 3 // 2
        rate_rows = (kinds * SUB, LANES)
        high = pitch_of(width) * height
        other = [across(features)]
        proj_row2 = across(proj_row)
        wide = jax.ShapeDtypeStruct((cells, LANES), F32)
        rates = jax.ShapeDtypeStruct(rate_rows, F32)
        entries = log_table.shape[0]
        xa, xb, la, lb, half, rates, skips, entry, marks = call(
            lambda *r: own_kernel((height, width), *r),
            [rate, features, decay_idx, log_table, proj_row, skip],
            [wide] * 5
            + [
                rates,
                jax.ShapeDtypeStruct((2 * SUB, LANES), F32),
                jax.ShapeDtypeStruct((height, LANES), F32),
                jax.ShapeDtypeStruct((3 * entries, 2 * LANES), BF16),
            ],
            [(high, LANES)] * 3 + [jax.ShapeDtypeStruct((cells, LANES), BF16)],
            8 << 20,
            left=True,
        )
        if tiles == 2:
            note, ta, tb, sa, sb, cf = call(
                lambda *r: tile_kernel((height, width), *r),
                [other[0], proj_row2, xa, xb, la, lb, half, rates, skips, entry],
                [jax.ShapeDtypeStruct(((kinds + 6) * height, LANES), BF16)] + [wide] * 5,
                [(high, LANES)] + [(states * cells, LANES)] * 2,
                16 << 20,
            )
            came = lax.ppermute(note, "cols", swap)
            brings = call(
                lambda *r: weigh_kernel(*r),
                [cf, sa, sb, rates],
                jax.ShapeDtypeStruct((kinds * cells, LANES), F32),
                [(states * cells, LANES)],
                16 << 20,
            )
            sent = call(
                lambda *r: join_kernel((strips, height, width, strip), dest, *r),
                [note, came, ta, tb, brings, entry, marks, rates],
                [block] * strips,
                [((width + 2) * height, LANES)] * 2,
                8 << 20,
            )
        else:
            rounds = [[(i, (i + d) % tiles) for i in range(tiles)] for d in range(1, tiles)]
            own = [features] + [lax.ppermute(features, "cols", pairs) for pairs in rounds]
            idx = [decay_idx] + [lax.ppermute(decay_idx, "cols", pairs) for pairs in rounds]
            other += [across(f) for f in own[1:]]
            sent = call(
                lambda *r: row_kernel((tiles, strips, height, width, strip), dest, *r),
                [rate, *own, *other, *idx, log_table, proj_row, proj_row2, skip],
                [block] * strips,
                [(tiles * high, LANES)] * 3
                + [(tiles * cells, LANES)] * 5
                + [(states * tiles * cells, LANES), (states * cells, LANES)]
                + [((width + 2) * height, LANES)] * 2
                + [rate_rows, (height, LANES), jax.ShapeDtypeStruct((cells, LANES), BF16)],
                40 << 20,
            )
        got = exchange(sent)
        back = jax.ShapeDtypeStruct((height * strip * 3 // 2, LANES), BF16)
        dims = strips, height, strip
        apart = jax.ShapeDtypeStruct((strip * pitch_of(total), LANES), F32)
        mid_a, mid_b, part = call(
            lambda *r: conv_kernel(dims, dest, *r),
            [*got, conv_w, bias, proj_col],
            [apart] * 3,
            [(count * (total + 2 * SUB), LANES)] * 2,
            8 << 20,
        )
        part2 = across(part)
        wide = jax.ShapeDtypeStruct((total * strip, LANES), F32)
        xa, xb, decay = call(
            lambda *r: decay_kernel(dims, dest, *r),
            [*got, mid_a, mid_b, marks, rates],
            [wide] * 2 + [jax.ShapeDtypeStruct((kinds * total * strip, LANES), F32)],
            [apart] * 2 + [jax.ShapeDtypeStruct((total * strip, LANES), BF16)],
            8 << 20,
        )
        sent = call(
            lambda *r: column_kernel(dims, dest, *r),
            [part, part2, xa, xb, decay, skips],
            [back] * strips,
            [wide] * 3 + [(states * total * strip, LANES)] * 2,
            20 << 20,
        )
        got = exchange(sent)
        return call(
            lambda *r: gate_kernel((strips, height, width, strip), dest, *r),
            [*got, gate],
            jax.ShapeDtypeStruct(features.shape, BF16),
            [(cells, LANES)] * 2,
            8 << 20,
        )

    return shards


def solution(mesh):
    placed = (
        P(("slides", "rows"), "cols", "chan"),
        P(("slides", "rows"), "cols", "chan"),
        P(("slides", "rows"), "cols"),
        P(None, "chan"),
        P(),
        P("chan", None),
        P("chan", None),
        P(None, None, "chan"),
        P("chan"),
        P("chan"),
    )
    shards = make_shards(mesh.shape["rows"], mesh.shape["cols"])

    return jax.shard_map(
        shards, mesh=mesh, in_specs=placed, out_specs=P(("slides", "rows"), "cols", "chan"), check_vma=False
    )
```
